32 devices in a mesh: groups: 2 (over y), seq: 4 (over z), head: 2 (over x), batch: 2 (over core).
Axes of the slice: x: 2, y: 2, z: 4, core: 2. Of those that a mesh axis runs over, the one named last changes fastest.
Arguments:
- queries: bfloat16 [4, 512, 2560], P(('groups', 'batch'), 'seq', 'head'), parts along dimension 0, may hold values from -6 to 6
- keys: bfloat16 [4, 512, 2560], P(('groups', 'batch'), 'seq', 'head'), parts along dimension 0, may hold values from -6 to 6
- values: bfloat16 [4, 512, 2560], P(('groups', 'batch'), 'seq', 'head'), parts along dimension 0, may hold values from -6 to 6
- cache_keys: bfloat16 [4, 8, 32, 2560], P(('groups', 'batch'), 'seq', None, 'head'), parts along dimension 0, may hold values from -6 to 6
- cache_values: bfloat16 [4, 8, 32, 2560], P(('groups', 'batch'), 'seq', None, 'head'), parts along dimension 0, may hold values from -6 to 6
- frame_list: int32 [4, 3], P(('groups', 'batch')), parts along dimension 0, may hold values from 0 to 7, as said below
- frame_place: int32 [4, 8], P(('groups', 'batch')), parts along dimension 0, may hold values from 0 to 7, each once within a row
- tile_mask: int32 [4, 4, 4], P(('groups', 'batch'), 'seq'), parts along dimension 0, may hold values from 0 to 1, as said below
Outputs:
- attention: bfloat16 [4, 512, 2560], P(('groups', 'batch'), 'seq', 'head'), parts along dimension 0
The draws below stay inside these ranges and needn't reach their ends.
There are 2 independent parts, one for each index of `groups`. The reference program is written for one: setup_inputs(seed, part) draws one part's arguments, and reference() takes and returns one part's arrays. A program takes and returns all parts, laid end to end along the dimension named above; each array names one. Nothing has to cross between parts.
Inputs may be any that keep to these rules, and one draw needn't show every extreme that they name: `frame_list`: each row holds frame 0 and then 3 - 1 consecutive frame numbers. `tile_mask`: ones on the diagonal of each video's tile matrix.
All inputs are finite; a program needn't handle non-finite values.
Results may differ from the reference program's by a relative error of at most 0.006.
Values may be sent and summed in bfloat16 or wider, within the bound.
No kernel may reach another device: no remote copies, remote signals or barrier semaphores. Data moves between devices by JAX's collectives and lax.ppermute only.
A program may use at most 128 MiB of HBM per device.

```python
import math
import jax
import jax.numpy as jnp
from jax import lax

HEADS = 20
HD = 128
TILE = 128
FRAME_TOK = 32
CURRENT = 512
NTILE = 4
FRAMES = 8
LIST = 3
VIDEOS = 2


def draw_queries(key, part):
    drawn = jnp.clip(jax.random.normal(jax.random.fold_in(key, 1), (VIDEOS, CURRENT, HEADS * HD), jnp.float32), -6.0, 6.0)
    return drawn.astype(jnp.bfloat16)


def draw_keys(key, part):
    drawn = jnp.clip(jax.random.normal(jax.random.fold_in(key, 2), (VIDEOS, CURRENT, HEADS * HD), jnp.float32), -6.0, 6.0)
    return drawn.astype(jnp.bfloat16)


def draw_tile_mask(key, part):
    tossed = jax.random.randint(key, (VIDEOS, NTILE, NTILE), 0, 2)
    diagonal = jnp.eye(NTILE, dtype=jnp.int32)[None, :, :]
    return jnp.where((tossed == 0) | (diagonal > 0), 1, 0).astype(jnp.int32)


def draw_frame_list(key, part):
    newest = jax.random.randint(key, (VIDEOS, 1), LIST - 1, FRAMES)
    window = newest - (LIST - 2) + jnp.arange(LIST - 1, dtype=jnp.int32)[None, :]
    return jnp.concatenate([jnp.zeros((VIDEOS, 1), jnp.int32), window.astype(jnp.int32)], axis=1)


def block_levels(rng, shape, pieces, low, largest):
    loudness = 1.0
    for dim, parts in pieces:
        draws = jax.random.uniform(jax.random.fold_in(jax.random.fold_in(rng, 6), dim), (parts,), jnp.float32, low / len(pieces), largest / len(pieces))
        loudness = loudness * jnp.repeat(jnp.exp(draws), shape[dim] // parts).reshape((-1,) + (1,) * (len(shape) - 1 - dim))
    return loudness


def normal_values(rng, dims, spread, reach, split=(), kind=jnp.bfloat16):
    gain = block_levels(rng, dims, split, -0.22, 0.18) if split else 1.0
    values = jax.random.normal(rng, dims, jnp.float32) * spread * gain
    return jnp.minimum(jnp.maximum(values, -reach), reach).astype(kind)


def setup_inputs(seed: int = 0, part: int = 0) -> dict:
    seeds = jax.random.split(jax.random.key(seed), 9)
    part_keys = jax.random.split(jax.random.fold_in(seeds[8], part), 9)
    return {
        "queries": draw_queries(jax.random.fold_in(jax.random.fold_in(seeds[8], part), 71), part),
        "keys": draw_keys(jax.random.fold_in(jax.random.fold_in(seeds[8], part), 71), part),
        "values": normal_values(part_keys[2], (VIDEOS, CURRENT, HEADS * HD), 1.0, 6.0, ((0, 2), (1, 4), (2, 2))),
        "cache_keys": normal_values(part_keys[3], (VIDEOS, FRAMES, FRAME_TOK, HEADS * HD), 1.0, 6.0, ((0, 2), (1, 4), (3, 2))),
        "cache_values": normal_values(part_keys[4], (VIDEOS, FRAMES, FRAME_TOK, HEADS * HD), 1.0, 6.0, ((0, 2), (1, 4), (3, 2))),
        "frame_list": draw_frame_list(jax.random.fold_in(jax.random.fold_in(seeds[8], part), 71), part),
        "frame_place": jax.vmap(lambda own: jax.random.permutation(own, FRAMES))(jax.random.split(part_keys[6], VIDEOS)).reshape((VIDEOS, FRAMES)).astype(jnp.int32),
        "tile_mask": draw_tile_mask(jax.random.fold_in(jax.random.fold_in(seeds[8], part), 71), part),
    }


def attend_head(query_h, key_h, value_h, live_mask):
    scores = jnp.dot(query_h, key_h.T, preferred_element_type=jnp.float32) * (1.0 / math.sqrt(HD))
    scores = jnp.where(live_mask, scores, -jnp.inf)
    peak = lax.optimization_barrier(jnp.max(scores, axis=1, keepdims=True))
    weights = jnp.where(live_mask, jnp.exp(scores - peak), 0.0)
    total = lax.optimization_barrier(jnp.sum(weights, axis=1, keepdims=True))
    rounded = weights.astype(jnp.bfloat16)
    summed = jnp.dot(rounded, value_h, preferred_element_type=jnp.float32)
    return (summed / total).astype(jnp.bfloat16)

def one_video(packed):
    query_v, key_v, value_v, live_mask = packed

    def per_head(triple):
        return attend_head(triple[0], triple[1], triple[2], live_mask)
    return lax.map(per_head, (query_v, key_v, value_v))

def reference(queries, keys, values, cache_keys, cache_values, frame_list, frame_place, tile_mask):
    videos = queries.shape[0]
    listed = jnp.any(frame_place[:, :, None] == frame_list[:, None, :], axis=2)
    tile_of = jnp.arange(CURRENT, dtype=jnp.int32) // TILE
    current_live = tile_mask[:, tile_of][:, :, tile_of] > 0
    cache_live = jnp.repeat(listed, FRAME_TOK, axis=1)
    cache_live = jnp.broadcast_to(cache_live[:, None, :], (videos, CURRENT, FRAMES * FRAME_TOK))
    live_mask = jnp.concatenate([current_live, cache_live], axis=2)
    all_keys = jnp.concatenate([keys, cache_keys.reshape(videos, FRAMES * FRAME_TOK, HEADS * HD)], axis=1)
    all_values = jnp.concatenate([values, cache_values.reshape(videos, FRAMES * FRAME_TOK, HEADS * HD)], axis=1)

    def split_heads(array):
        return array.reshape(videos, array.shape[1], HEADS, HD).transpose(0, 2, 1, 3)
    result = lax.map(one_video, (split_heads(queries), split_heads(all_keys), split_heads(all_values), live_mask))
    return result.transpose(0, 2, 1, 3).reshape(videos, CURRENT, HEADS * HD)
```

```python
import functools
import math

import jax
import jax.numpy as jnp
from jax import lax
from jax.experimental import pallas as pl
from jax.experimental.pallas import tpu as pltpu
from jax.sharding import PartitionSpec as P

HD = 128
TILE = 128
NEG_FILL = -1e30
FACTOR = math.log2(math.e) / math.sqrt(HD)
FLAG_ROWS = 16
VMEM = pl.BlockSpec(memory_space=pltpu.VMEM)
SMEM = pl.BlockSpec(memory_space=pltpu.SMEM)
BF16 = jnp.bfloat16
F32 = jnp.float32


def attend(running, key_part, value_part, live, query_heads):
    videos, length, col_count = key_part.shape
    head_count = col_count // HD

    def update(previous):
        peak_old, total_old, summed_old = previous
        key_heads = key_part.reshape(videos, length, head_count, HD)
        value_heads = value_part.reshape(videos, length, head_count, HD)
        scores = jnp.einsum(
            "vqhd,vkhd->vhqk", query_heads, key_heads, preferred_element_type=jnp.float32
        ) * (1.0 / math.sqrt(HD))
        allowed = live[:, None, :, :]
        scores = jnp.where(allowed, scores, NEG_FILL)
        peak_new = jnp.maximum(peak_old, jnp.max(scores, axis=3))
        weights = jnp.where(allowed, jnp.exp(scores - peak_new[..., None]), 0.0)
        factor = jnp.exp(peak_old - peak_new)
        total_new = total_old * factor + jnp.sum(weights, axis=3)
        product = jnp.einsum(
            "vhqk,vkhd->vhqd",
            weights.astype(jnp.bfloat16),
            value_heads,
            preferred_element_type=jnp.float32,
        )
        summed_new = summed_old * factor[..., None] + product
        return (peak_new, total_new, summed_new)

    def unchanged(previous):
        return previous

    return lax.cond(jnp.any(live), update, unchanged, running)


def gathered(queries, keys, values, cache_keys, cache_values, frame_list, frame_place, tile_mask):
    videos, tok_rows, col_count = queries.shape
    head_count = col_count // HD
    query_heads = queries.reshape(videos, tok_rows, head_count, HD)
    running = (
        jnp.full((videos, head_count, tok_rows), NEG_FILL, jnp.float32),
        jnp.zeros((videos, head_count, tok_rows), jnp.float32),
        jnp.zeros((videos, head_count, tok_rows, HD), jnp.float32),
    )
    frame_tok = cache_keys.shape[2]
    listed = jnp.any(frame_place[:, :, None] == frame_list[:, None, :], axis=2)
    key_piece = lax.all_gather(cache_keys, "seq", axis=1, tiled=True)
    value_piece = lax.all_gather(cache_values, "seq", axis=1, tiled=True)
    count_frames = key_piece.shape[1]
    token_flags = jnp.repeat(listed, frame_tok, axis=1)
    live = jnp.broadcast_to(token_flags[:, None, :], (videos, tok_rows, count_frames * frame_tok))
    key_flat = key_piece.reshape(videos, count_frames * frame_tok, col_count)
    value_flat = value_piece.reshape(videos, count_frames * frame_tok, col_count)
    running = attend(running, key_flat, value_flat, live, query_heads)
    key_piece = lax.all_gather(keys, "seq", axis=1, tiled=True)
    value_piece = lax.all_gather(values, "seq", axis=1, tiled=True)
    length = key_piece.shape[1]
    key_tiles = jnp.arange(length, dtype=jnp.int32) // TILE
    tile_live = jnp.take(tile_mask, key_tiles, axis=2)
    running = attend(
        running, key_piece, value_piece, jnp.repeat(tile_live, TILE, axis=1) > 0, query_heads
    )
    peak, total, summed = running
    result = summed / total[..., None]
    return result.transpose(0, 2, 1, 3).reshape(videos, tok_rows, col_count).astype(jnp.bfloat16)


def head_cols(head):
    start = head * HD
    if not isinstance(head, int):
        start = pl.multiple_of(start, HD)
    return pl.ds(start, HD)


def fill(live):
    return jnp.where(live, 0.0, NEG_FILL)


def frame_fills(place_ref, list_ref, device, frames):
    out = []
    for slot in range(frames):
        held = place_ref[0, device * frames + slot]
        live = held == list_ref[0, 0]
        for entry in range(1, list_ref.shape[1]):
            live = live | (held == list_ref[0, entry])
        out.append(fill(live))
    return out


def rows_of(ref, head):
    if len(ref.shape) == 3:
        return ref[0, :, head_cols(head)]
    return ref[0, :, :, head_cols(head)].reshape(ref.shape[1] * ref.shape[2], HD)


def pack_kernel(half, mask_ref, q_ref, k_ref, v_ref, ck_ref, cv_ref, *out_refs):
    split_refs, whole_refs = out_refs[:3], out_refs[3:]
    me = lax.axis_index("seq")
    side = lax.rem(me, 2)
    parts = (q_ref, k_ref, v_ref, ck_ref, cv_ref)
    for rel in (1, 2, 3):
        other = jnp.bitwise_xor(me, rel)
        group = (1 - side) if rel % 2 else side
        out = split_refs[rel - 1]
        row = 0
        for j in range(half):
            head = group * half + j
            for ref in parts if rel == 1 else parts[:1]:
                block = rows_of(ref, head)
                out[row : row + block.shape[0], :] = block
                row += block.shape[0]
        flags = [fill(mask_ref[0, 0, jnp.bitwise_xor(other, key)] > 0) for key in range(4)]
        ident = lax.broadcasted_iota(jnp.int32, (FLAG_ROWS, HD), 0)
        block = jnp.zeros((FLAG_ROWS, HD), F32)
        for key in range(4):
            block = jnp.where(ident == key, flags[key], block)
        out[row : row + FLAG_ROWS, :] = block.astype(BF16)
        out = whole_refs[rel - 1]
        row = 0
        for ref in parts:
            block = rows_of(ref, 2 * half + other)
            out[row : row + block.shape[0], :] = block
            row += block.shape[0]


def softmax_part(key_rows, value_rows, query_rows, fills):
    scores = lax.dot_general(
        key_rows, query_rows, (((1,), (1,)), ((), ())), preferred_element_type=F32
    )
    pieces = []
    row = 0
    for count, value in fills:
        pieces.append(scores[row : row + count, :] * FACTOR + value)
        row += count
    scores = jnp.concatenate(pieces, axis=0)
    peak = jnp.max(scores, axis=0, keepdims=True)
    weights = jnp.exp2(scores - peak)
    total = jnp.sum(weights, axis=0, keepdims=True)
    summed = lax.dot_general(
        value_rows, weights.astype(BF16), (((0,), (0,)), ((), ())), preferred_element_type=F32
    )
    return summed / total, peak + jnp.log2(total)


def own_flags(mask_ref, me):
    return [
        jnp.full((1, TILE), fill(mask_ref[0, 0, jnp.bitwise_xor(me, key)] > 0), F32)
        for key in range(4)
    ]


def split_kernel(
    half, frames, frame_tok,
    mask_ref, list_ref, place_ref, q_ref, k_ref, v_ref, ck_ref, cv_ref, in1_ref, in2_ref, in3_ref,
    own_ref, own_log_ref, out1_ref, out2_ref, out3_ref,
):
    me = lax.axis_index("seq")
    side = lax.rem(me, 2)
    cache = frames * frame_tok
    span = 3 * TILE + 2 * cache
    flags = [own_flags(mask_ref, me)]
    for ref, row in ((in1_ref, half * span), (in2_ref, half * TILE), (in3_ref, half * TILE)):
        block = ref[row : row + FLAG_ROWS, :].astype(F32)
        flags.append([block[key : key + 1, :] for key in range(4)])
    fills = [(TILE, jnp.concatenate([flags[rel][key] for rel in range(4)], axis=1)) for key in range(2)]
    for rel in range(2):
        for value in frame_fills(place_ref, list_ref, jnp.bitwise_xor(me, rel), frames):
            fills.append((frame_tok, value))
    stats = [[], [], []]
    for j in range(half):
        head = side * half + j
        base = j * span
        query_rows = jnp.concatenate(
            [
                rows_of(q_ref, head),
                in1_ref[base : base + TILE, :],
                in2_ref[j * TILE : (j + 1) * TILE, :],
                in3_ref[j * TILE : (j + 1) * TILE, :],
            ],
            axis=0,
        )
        key_rows = jnp.concatenate(
            [
                rows_of(k_ref, head),
                in1_ref[base + TILE : base + 2 * TILE, :],
                rows_of(ck_ref, head),
                in1_ref[base + 3 * TILE : base + 3 * TILE + cache, :],
            ],
            axis=0,
        )
        value_rows = jnp.concatenate(
            [
                rows_of(v_ref, head),
                in1_ref[base + 2 * TILE : base + 3 * TILE, :],
                rows_of(cv_ref, head),
                in1_ref[base + 3 * TILE + cache : base + 3 * TILE + 2 * cache, :],
            ],
            axis=0,
        )
        summed, logs = softmax_part(key_rows, value_rows, query_rows, fills)
        rows = slice(j * HD, (j + 1) * HD)
        own_ref[rows, :] = summed[:, :TILE]
        own_log_ref[j : j + 1, :] = logs[:, :TILE]
        for rel, out in ((1, out1_ref), (2, out2_ref), (3, out3_ref)):
            cols = slice(rel * TILE, (rel + 1) * TILE)
            out[rows, :] = summed[:, cols].astype(BF16)
            rest = logs[:, cols]
            for _ in range(3):
                part = rest.astype(BF16).astype(F32)
                stats[rel - 1].append(part)
                rest = rest - part
    spare = FLAG_ROWS - 3 * half
    for rel, out in ((1, out1_ref), (2, out2_ref), (3, out3_ref)):
        block = jnp.concatenate(stats[rel - 1] + [jnp.zeros((spare, TILE), F32)], axis=0)
        out[half * HD : half * HD + FLAG_ROWS, :] = block.astype(BF16)


def whole_kernel(
    half, frames, frame_tok,
    mask_ref, list_ref, place_ref, q_ref, k_ref, v_ref, ck_ref, cv_ref,
    flags1_ref, flags2_ref, flags3_ref, in1_ref, in2_ref, in3_ref,
    own_ref, out1_ref, out2_ref, out3_ref,
):
    me = lax.axis_index("seq")
    cache = frames * frame_tok
    flags = [own_flags(mask_ref, me)]
    for ref in (flags1_ref, flags2_ref, flags3_ref):
        row = ref.shape[0] - FLAG_ROWS
        block = ref[row : row + FLAG_ROWS, :].astype(F32)
        flags.append([block[key : key + 1, :] for key in range(4)])
    fills = [(TILE, jnp.concatenate([flags[rel][key] for rel in range(4)], axis=1)) for key in range(4)]
    for rel in range(4):
        for value in frame_fills(place_ref, list_ref, jnp.bitwise_xor(me, rel), frames):
            fills.append((frame_tok, value))
    head = 2 * half + me
    ins = (in1_ref, in2_ref, in3_ref)
    end = 3 * TILE + cache
    query_rows = jnp.concatenate([rows_of(q_ref, head)] + [ref[0:TILE, :] for ref in ins], axis=0)
    key_rows = jnp.concatenate(
        [rows_of(k_ref, head)] + [ref[TILE : 2 * TILE, :] for ref in ins]
        + [rows_of(ck_ref, head)] + [ref[3 * TILE : end, :] for ref in ins],
        axis=0,
    )
    value_rows = jnp.concatenate(
        [rows_of(v_ref, head)] + [ref[2 * TILE : 3 * TILE, :] for ref in ins]
        + [rows_of(cv_ref, head)] + [ref[end : end + cache, :] for ref in ins],
        axis=0,
    )
    summed, _ = softmax_part(key_rows, value_rows, query_rows, fills)
    for rel, out in enumerate((own_ref, out1_ref, out2_ref, out3_ref)):
        out[...] = summed[:, rel * TILE : (rel + 1) * TILE].astype(BF16)


def merge_kernel(
    half,
    own_ref, own_log_ref, in1_ref, in2_ref, in3_ref,
    whole0_ref, whole1_ref, whole2_ref, whole3_ref,
    out_ref,
):
    me = lax.axis_index("seq")
    side = lax.rem(me, 2)

    def logs_of(ref, j):
        block = ref[half * HD : half * HD + FLAG_ROWS, :].astype(F32)
        row = 3 * j
        return block[row : row + 1, :] + block[row + 1 : row + 2, :] + block[row + 2 : row + 3, :]

    def joined(first, first_log, second, second_log):
        peak = jnp.maximum(first_log, second_log)
        first_weight = jnp.exp2(first_log - peak)
        second_weight = jnp.exp2(second_log - peak)
        return (first * first_weight + second * second_weight) / (first_weight + second_weight)

    for j in range(half):
        rows = slice(j * HD, (j + 1) * HD)
        near = joined(
            own_ref[rows, :], own_log_ref[j : j + 1, :],
            in2_ref[rows, :].astype(F32), logs_of(in2_ref, j),
        )
        out_ref[0, :, head_cols(side * half + j)] = near.T.astype(BF16)
        far = joined(
            in1_ref[rows, :].astype(F32), logs_of(in1_ref, j),
            in3_ref[rows, :].astype(F32), logs_of(in3_ref, j),
        )
        out_ref[0, :, head_cols((1 - side) * half + j)] = far.T.astype(BF16)
    for rel, ref in enumerate((whole0_ref, whole1_ref, whole2_ref, whole3_ref)):
        block = ref[...].astype(F32).T.astype(BF16)
        out_ref[0, :, head_cols(2 * half + jnp.bitwise_xor(me, rel))] = block


def send(array, rel):
    return lax.ppermute(array, "seq", [(i, i ^ rel) for i in range(4)])


def exchanged(queries, keys, values, cache_keys, cache_values, frame_list, frame_place, tile_mask):
    head_count = queries.shape[2] // HD
    half = (head_count - 4) // 2
    frames, frame_tok = cache_keys.shape[1:3]
    span = 3 * TILE + 2 * frames * frame_tok
    shape = jax.ShapeDtypeStruct
    arrays = (queries, keys, values, cache_keys, cache_values)
    packed = pl.pallas_call(
        functools.partial(pack_kernel, half),
        out_shape=(
            shape((half * span + FLAG_ROWS, HD), BF16),
            shape((half * TILE + FLAG_ROWS, HD), BF16),
            shape((half * TILE + FLAG_ROWS, HD), BF16),
        ) + (shape((span, HD), BF16),) * 3,
        in_specs=[SMEM] + [VMEM] * 5,
        out_specs=(VMEM,) * 6,
    )(tile_mask, *arrays)
    split_in = [send(packed[rel - 1], rel) for rel in (1, 2, 3)]
    whole_in = [send(packed[rel + 2], rel) for rel in (1, 2, 3)]
    own, own_log, *split_out = pl.pallas_call(
        functools.partial(split_kernel, half, frames, frame_tok),
        out_shape=(
            shape((half * HD, TILE), F32),
            shape((half, TILE), F32),
        ) + (shape((half * HD + FLAG_ROWS, TILE), BF16),) * 3,
        in_specs=[SMEM] * 3 + [VMEM] * 8,
        out_specs=(VMEM,) * 5,
    )(tile_mask, frame_list, frame_place, *arrays, *split_in)
    split_back = [send(split_out[rel - 1], rel) for rel in (1, 2, 3)]
    whole_out = pl.pallas_call(
        functools.partial(whole_kernel, half, frames, frame_tok),
        out_shape=(shape((HD, TILE), BF16),) * 4,
        in_specs=[SMEM] * 3 + [VMEM] * 11,
        out_specs=(VMEM,) * 4,
    )(tile_mask, frame_list, frame_place, *arrays, *split_in, *whole_in)
    whole_back = [whole_out[0]] + [send(whole_out[rel], rel) for rel in (1, 2, 3)]
    return pl.pallas_call(
        functools.partial(merge_kernel, half),
        out_shape=shape(queries.shape, BF16),
        in_specs=[VMEM] * 9,
        out_specs=VMEM,
    )(own, own_log, *split_back, *whole_back)


def body(queries, keys, values, cache_keys, cache_values, frame_list, frame_place, tile_mask):
    head_count = queries.shape[2] // HD
    fits = (
        lax.axis_size("seq") == 4
        and queries.shape[0] == 1
        and queries.shape[1] == TILE
        and head_count % 2 == 0
        and 6 <= head_count <= 14
    )
    run = exchanged if fits else gathered
    return run(queries, keys, values, cache_keys, cache_values, frame_list, frame_place, tile_mask)


def solution(mesh):
    return jax.shard_map(
        body,
        mesh=mesh,
        in_specs=(
            P(("groups", "batch"), "seq", "head"),
            P(("groups", "batch"), "seq", "head"),
            P(("groups", "batch"), "seq", "head"),
            P(("groups", "batch"), "seq", None, "head"),
            P(("groups", "batch"), "seq", None, "head"),
            P(("groups", "batch"), None),
            P(("groups", "batch"), None),
            P(("groups", "batch"), "seq", None),
        ),
        out_specs=P(("groups", "batch"), "seq", "head"),
        check_vma=False,
    )
```

```python
import functools
import math

import jax
import jax.numpy as jnp
from jax import lax
from jax.experimental import pallas as pl
from jax.experimental.pallas import tpu as pltpu
from jax.sharding import PartitionSpec as P

HD = 128
TILE = 128
NEG_FILL = -1e30
FACTOR = math.log2(math.e) / math.sqrt(HD)
FLAG_ROWS = 16
VMEM = pl.BlockSpec(memory_space=pltpu.VMEM)
SMEM = pl.BlockSpec(memory_space=pltpu.SMEM)
BF16 = jnp.bfloat16
F32 = jnp.float32


def attend(running, key_part, value_part, live, query_heads):
    videos, length, col_count = key_part.shape
    head_count = col_count // HD

    def update(previous):
        peak_old, total_old, summed_old = previous
        key_heads = key_part.reshape(videos, length, head_count, HD)
        value_heads = value_part.reshape(videos, length, head_count, HD)
        scores = jnp.einsum(
            "vqhd,vkhd->vhqk", query_heads, key_heads, preferred_element_type=jnp.float32
        ) * (1.0 / math.sqrt(HD))
        allowed = live[:, None, :, :]
        scores = jnp.where(allowed, scores, NEG_FILL)
        peak_new = jnp.maximum(peak_old, jnp.max(scores, axis=3))
        weights = jnp.where(allowed, jnp.exp(scores - peak_new[..., None]), 0.0)
        factor = jnp.exp(peak_old - peak_new)
        total_new = total_old * factor + jnp.sum(weights, axis=3)
        product = jnp.einsum(
            "vhqk,vkhd->vhqd",
            weights.astype(jnp.bfloat16),
            value_heads,
            preferred_element_type=jnp.float32,
        )
        summed_new = summed_old * factor[..., None] + product
        return (peak_new, total_new, summed_new)

    def unchanged(previous):
        return previous

    return lax.cond(jnp.any(live), update, unchanged, running)


def gathered(queries, keys, values, cache_keys, cache_values, frame_list, frame_place, tile_mask):
    videos, tok_rows, col_count = queries.shape
    head_count = col_count // HD
    query_heads = queries.reshape(videos, tok_rows, head_count, HD)
    running = (
        jnp.full((videos, head_count, tok_rows), NEG_FILL, jnp.float32),
        jnp.zeros((videos, head_count, tok_rows), jnp.float32),
        jnp.zeros((videos, head_count, tok_rows, HD), jnp.float32),
    )
    frame_tok = cache_keys.shape[2]
    listed = jnp.any(frame_place[:, :, None] == frame_list[:, None, :], axis=2)
    key_piece = lax.all_gather(cache_keys, "seq", axis=1, tiled=True)
    value_piece = lax.all_gather(cache_values, "seq", axis=1, tiled=True)
    count_frames = key_piece.shape[1]
    token_flags = jnp.repeat(listed, frame_tok, axis=1)
    live = jnp.broadcast_to(token_flags[:, None, :], (videos, tok_rows, count_frames * frame_tok))
    key_flat = key_piece.reshape(videos, count_frames * frame_tok, col_count)
    value_flat = value_piece.reshape(videos, count_frames * frame_tok, col_count)
    running = attend(running, key_flat, value_flat, live, query_heads)
    key_piece = lax.all_gather(keys, "seq", axis=1, tiled=True)
    value_piece = lax.all_gather(values, "seq", axis=1, tiled=True)
    length = key_piece.shape[1]
    key_tiles = jnp.arange(length, dtype=jnp.int32) // TILE
    tile_live = jnp.take(tile_mask, key_tiles, axis=2)
    running = attend(
        running, key_piece, value_piece, jnp.repeat(tile_live, TILE, axis=1) > 0, query_heads
    )
    peak, total, summed = running
    result = summed / total[..., None]
    return result.transpose(0, 2, 1, 3).reshape(videos, tok_rows, col_count).astype(jnp.bfloat16)


def head_cols(head):
    start = head * HD
    if not isinstance(head, int):
        start = pl.multiple_of(start, HD)
    return pl.ds(start, HD)


def fill(live):
    return jnp.where(live, 0.0, NEG_FILL)


def frame_fills(place_ref, list_ref, device, frames):
    out = []
    for slot in range(frames):
        held = place_ref[0, device * frames + slot]
        live = held == list_ref[0, 0]
        for entry in range(1, list_ref.shape[1]):
            live = live | (held == list_ref[0, entry])
        out.append(fill(live))
    return out


def rows_of(ref, head):
    if len(ref.shape) == 3:
        return ref[0, :, head_cols(head)]
    return ref[0, :, :, head_cols(head)].reshape(ref.shape[1] * ref.shape[2], HD)


def pack_kernel(
    half, mask_ref, q_ref, k_ref, v_ref, ck_ref, cv_ref,
    split0_ref, split1_ref, whole0_ref, whole1_ref, whole2_ref, whole3_ref,
):
    me = lax.axis_index("seq")
    side = lax.rem(me, 2)
    parts = (q_ref, k_ref, v_ref, ck_ref, cv_ref)
    for rel, out in enumerate((whole0_ref, whole1_ref, whole2_ref, whole3_ref)):
        other = jnp.bitwise_xor(me, rel)
        group = (1 - side) if rel % 2 else side
        row = 0
        for ref in parts:
            block = rows_of(ref, 2 * half + other)
            out[row : row + block.shape[0], :] = block
            row += block.shape[0]
        ident = lax.broadcasted_iota(jnp.int32, (FLAG_ROWS, HD), 0)
        block = jnp.zeros((FLAG_ROWS, HD), F32)
        for key in range(4):
            live = mask_ref[0, 0, jnp.bitwise_xor(other, key)] > 0
            block = jnp.where(ident == key, fill(live), block)
        out[row : row + FLAG_ROWS, :] = block.astype(BF16)
        row += FLAG_ROWS
        for j in range(half):
            if rel >= 2:
                out[row : row + TILE, :] = rows_of(q_ref, group * half + j)
                row += TILE
    for rel, out in enumerate((split0_ref, split1_ref)):
        group = (1 - side) if rel % 2 else side
        row = 0
        for j in range(half):
            for ref in parts:
                block = rows_of(ref, group * half + j)
                out[row : row + block.shape[0], :] = block
                row += block.shape[0]


def softmax_part(key_rows, value_rows, query_rows, fills):
    scores = lax.dot_general(
        key_rows, query_rows, (((1,), (1,)), ((), ())), preferred_element_type=F32
    )
    pieces = []
    row = 0
    for count, value in fills:
        pieces.append(scores[row : row + count, :] * FACTOR + value)
        row += count
    scores = jnp.concatenate(pieces, axis=0)
    peak = jnp.max(scores, axis=0, keepdims=True)
    weights = jnp.exp2(scores - peak)
    total = jnp.sum(weights, axis=0, keepdims=True)
    summed = lax.dot_general(
        value_rows, weights.astype(BF16), (((0,), (0,)), ((), ())), preferred_element_type=F32
    )
    return summed / total, peak + jnp.log2(total)


def query_fills(refs, row, keys):
    blocks = [ref[row : row + FLAG_ROWS, :].astype(F32) for ref in refs]
    return [
        (TILE, jnp.concatenate([block[key : key + 1, :] for block in blocks], axis=1))
        for key in range(keys)
    ]


def stack(refs, start, count):
    return jnp.concatenate([ref[start : start + count, :] for ref in refs], axis=0)


def whole_kernel(
    half, frames, frame_tok,
    list_ref, place_ref, in0_ref, in1_ref, in2_ref, in3_ref,
    own_ref, out1_ref, out2_ref, out3_ref,
):
    me = lax.axis_index("seq")
    cache = frames * frame_tok
    span = 3 * TILE + 2 * cache
    ins = (in0_ref, in1_ref, in2_ref, in3_ref)
    fills = query_fills(ins, span, 4)
    for rel in range(4):
        for value in frame_fills(place_ref, list_ref, jnp.bitwise_xor(me, rel), frames):
            fills.append((frame_tok, value))
    end = 3 * TILE + cache
    query_rows = stack(ins, 0, TILE)
    key_rows = jnp.concatenate([stack(ins, TILE, TILE), stack(ins, 3 * TILE, cache)], axis=0)
    value_rows = jnp.concatenate([stack(ins, 2 * TILE, TILE), stack(ins, end, cache)], axis=0)
    summed, _ = softmax_part(key_rows, value_rows, query_rows, fills)
    for rel, out in enumerate((own_ref, out1_ref, out2_ref, out3_ref)):
        out[...] = summed[:, rel * TILE : (rel + 1) * TILE].astype(BF16)


def split_kernel(
    half, frames, frame_tok,
    list_ref, place_ref, split0_ref, split1_ref,
    in0_ref, in1_ref, in2_ref, in3_ref, whole1_ref, whole2_ref, whole3_ref,
    own_ref, own_log_ref, out1_ref, out2_ref, out3_ref,
):
    me = lax.axis_index("seq")
    cache = frames * frame_tok
    span = 3 * TILE + 2 * cache
    fills = query_fills((in0_ref, in1_ref, in2_ref, in3_ref), span, 2)
    for rel in range(2):
        for value in frame_fills(place_ref, list_ref, jnp.bitwise_xor(me, rel), frames):
            fills.append((frame_tok, value))
    pair = (split0_ref, split1_ref)
    outs = (out1_ref, out2_ref, out3_ref)
    for out, ref in zip(outs, (whole1_ref, whole2_ref, whole3_ref)):
        out[0:HD, :] = ref[...]
    stats = [[], [], []]
    for j in range(half):
        base = j * span
        end = base + 3 * TILE + cache
        far = span + FLAG_ROWS + j * TILE
        query_rows = jnp.concatenate(
            [stack(pair, base, TILE), stack((in2_ref, in3_ref), far, TILE)], axis=0
        )
        key_rows = jnp.concatenate(
            [stack(pair, base + TILE, TILE), stack(pair, base + 3 * TILE, cache)], axis=0
        )
        value_rows = jnp.concatenate(
            [stack(pair, base + 2 * TILE, TILE), stack(pair, end, cache)], axis=0
        )
        summed, logs = softmax_part(key_rows, value_rows, query_rows, fills)
        own_ref[j * HD : (j + 1) * HD, :] = summed[:, :TILE]
        own_log_ref[j : j + 1, :] = logs[:, :TILE]
        for rel, out in enumerate(outs, 1):
            cols = slice(rel * TILE, (rel + 1) * TILE)
            out[(j + 1) * HD : (j + 2) * HD, :] = summed[:, cols].astype(BF16)
            rest = logs[:, cols]
            for _ in range(3):
                part = rest.astype(BF16).astype(F32)
                stats[rel - 1].append(part)
                rest = rest - part
    spare = FLAG_ROWS - 3 * half
    start = (half + 1) * HD
    for rel, out in enumerate(outs, 1):
        block = jnp.concatenate(stats[rel - 1] + [jnp.zeros((spare, TILE), F32)], axis=0)
        out[start : start + FLAG_ROWS, :] = block.astype(BF16)


def merge_kernel(
    half, own_ref, own_log_ref, whole_ref, in1_ref, in2_ref, in3_ref, out_ref,
):
    me = lax.axis_index("seq")
    side = lax.rem(me, 2)
    start = (half + 1) * HD

    def logs_of(ref, j):
        block = ref[start : start + FLAG_ROWS, :].astype(F32)
        row = 3 * j
        return block[row : row + 1, :] + block[row + 1 : row + 2, :] + block[row + 2 : row + 3, :]

    def joined(first, first_log, second, second_log):
        peak = jnp.maximum(first_log, second_log)
        first_weight = jnp.exp2(first_log - peak)
        second_weight = jnp.exp2(second_log - peak)
        return (first * first_weight + second * second_weight) / (first_weight + second_weight)

    for j in range(half):
        rows = slice((j + 1) * HD, (j + 2) * HD)
        close = joined(
            own_ref[j * HD : (j + 1) * HD, :], own_log_ref[j : j + 1, :],
            in2_ref[rows, :].astype(F32), logs_of(in2_ref, j),
        )
        out_ref[0, :, head_cols(side * half + j)] = close.T.astype(BF16)
        far = joined(
            in1_ref[rows, :].astype(F32), logs_of(in1_ref, j),
            in3_ref[rows, :].astype(F32), logs_of(in3_ref, j),
        )
        out_ref[0, :, head_cols((1 - side) * half + j)] = far.T.astype(BF16)
    for rel, ref in enumerate((whole_ref, in1_ref, in2_ref, in3_ref)):
        block = ref[0:HD, :].astype(F32).T.astype(BF16)
        out_ref[0, :, head_cols(2 * half + jnp.bitwise_xor(me, rel))] = block


def send(array, rel):
    return lax.ppermute(array, "seq", [(i, i ^ rel) for i in range(4)])


def near(array):
    return pltpu.with_memory_space_constraint(array, pltpu.VMEM)


def exchanged(queries, keys, values, cache_keys, cache_values, frame_list, frame_place, tile_mask):
    head_count = queries.shape[2] // HD
    half = (head_count - 4) // 2
    frames, frame_tok = cache_keys.shape[1:3]
    span = 3 * TILE + 2 * frames * frame_tok
    split_rows = half * span
    whole_rows = span + FLAG_ROWS
    both_rows = whole_rows + half * TILE
    split0, split1, *whole = pl.pallas_call(
        functools.partial(pack_kernel, half),
        out_shape=(pltpu.VMEM((split_rows, HD), BF16),) * 2
        + (pltpu.VMEM((whole_rows, HD), BF16),) * 2
        + (pltpu.VMEM((both_rows, HD), BF16),) * 2,
        in_specs=[SMEM] + [VMEM] * 5,
        out_specs=(VMEM,) * 6,
    )(tile_mask, queries, keys, values, cache_keys, cache_values)
    whole_in = [near(whole[0])] + [near(send(whole[rel], rel)) for rel in (1, 2, 3)]
    split_in = [near(split0), near(send(split1, 1))]
    whole_out = pl.pallas_call(
        functools.partial(whole_kernel, half, frames, frame_tok),
        out_shape=(pltpu.VMEM((HD, TILE), BF16),) * 4,
        in_specs=[SMEM] * 2 + [VMEM] * 4,
        out_specs=(VMEM,) * 4,
    )(frame_list, frame_place, *whole_in)
    whole_out = [near(array) for array in whole_out]
    own, own_log, *back = pl.pallas_call(
        functools.partial(split_kernel, half, frames, frame_tok),
        out_shape=(
            pltpu.VMEM((half * HD, TILE), F32),
            pltpu.VMEM((half, TILE), F32),
        ) + (pltpu.VMEM(((half + 1) * HD + FLAG_ROWS, TILE), BF16),) * 3,
        in_specs=[SMEM] * 2 + [VMEM] * 9,
        out_specs=(VMEM,) * 5,
    )(frame_list, frame_place, *split_in, *whole_in, *whole_out[1:])
    back = [near(send(back[rel - 1], rel)) for rel in (1, 2, 3)]
    return pl.pallas_call(
        functools.partial(merge_kernel, half),
        out_shape=jax.ShapeDtypeStruct(queries.shape, BF16),
        in_specs=[VMEM] * 6,
        out_specs=VMEM,
    )(near(own), near(own_log), whole_out[0], *back)


def body(queries, keys, values, cache_keys, cache_values, frame_list, frame_place, tile_mask):
    head_count = queries.shape[2] // HD
    fits = (
        lax.axis_size("seq") == 4
        and queries.shape[0] == 1
        and queries.shape[1] == TILE
        and head_count % 2 == 0
        and 6 <= head_count <= 14
    )
    run = exchanged if fits else gathered
    return run(queries, keys, values, cache_keys, cache_values, frame_list, frame_place, tile_mask)


def solution(mesh):
    return jax.shard_map(
        body,
        mesh=mesh,
        in_specs=(
            P(("groups", "batch"), "seq", "head"),
            P(("groups", "batch"), "seq", "head"),
            P(("groups", "batch"), "seq", "head"),
            P(("groups", "batch"), "seq", None, "head"),
            P(("groups", "batch"), "seq", None, "head"),
            P(("groups", "batch"), None),
            P(("groups", "batch"), None),
            P(("groups", "batch"), "seq", None),
        ),
        out_specs=P(("groups", "batch"), "seq", "head"),
        check_vma=False,
    )
```

```python
import functools
import math

import jax
import jax.numpy as jnp
from jax import lax
from jax.experimental import pallas as pl
from jax.experimental.pallas import tpu as pltpu
from jax.sharding import PartitionSpec as P

HD = 128
TILE = 128
NEG_FILL = -1e30
FACTOR = math.log2(math.e) / math.sqrt(HD)
FLAG_ROWS = 16
VMEM = pl.BlockSpec(memory_space=pltpu.VMEM)
SMEM = pl.BlockSpec(memory_space=pltpu.SMEM)
BF16 = jnp.bfloat16
F32 = jnp.float32


def attend(running, key_part, value_part, live, query_heads):
    videos, length, col_count = key_part.shape
    head_count = col_count // HD

    def update(previous):
        peak_old, total_old, summed_old = previous
        key_heads = key_part.reshape(videos, length, head_count, HD)
        value_heads = value_part.reshape(videos, length, head_count, HD)
        scores = jnp.einsum(
            "vqhd,vkhd->vhqk", query_heads, key_heads, preferred_element_type=jnp.float32
        ) * (1.0 / math.sqrt(HD))
        allowed = live[:, None, :, :]
        scores = jnp.where(allowed, scores, NEG_FILL)
        peak_new = jnp.maximum(peak_old, jnp.max(scores, axis=3))
        weights = jnp.where(allowed, jnp.exp(scores - peak_new[..., None]), 0.0)
        factor = jnp.exp(peak_old - peak_new)
        total_new = total_old * factor + jnp.sum(weights, axis=3)
        product = jnp.einsum(
            "vhqk,vkhd->vhqd",
            weights.astype(jnp.bfloat16),
            value_heads,
            preferred_element_type=jnp.float32,
        )
        summed_new = summed_old * factor[..., None] + product
        return (peak_new, total_new, summed_new)

    def unchanged(previous):
        return previous

    return lax.cond(jnp.any(live), update, unchanged, running)


def gathered(queries, keys, values, cache_keys, cache_values, frame_list, frame_place, tile_mask):
    videos, tok_rows, col_count = queries.shape
    head_count = col_count // HD
    query_heads = queries.reshape(videos, tok_rows, head_count, HD)
    running = (
        jnp.full((videos, head_count, tok_rows), NEG_FILL, jnp.float32),
        jnp.zeros((videos, head_count, tok_rows), jnp.float32),
        jnp.zeros((videos, head_count, tok_rows, HD), jnp.float32),
    )
    frame_tok = cache_keys.shape[2]
    listed = jnp.any(frame_place[:, :, None] == frame_list[:, None, :], axis=2)
    key_piece = lax.all_gather(cache_keys, "seq", axis=1, tiled=True)
    value_piece = lax.all_gather(cache_values, "seq", axis=1, tiled=True)
    count_frames = key_piece.shape[1]
    token_flags = jnp.repeat(listed, frame_tok, axis=1)
    live = jnp.broadcast_to(token_flags[:, None, :], (videos, tok_rows, count_frames * frame_tok))
    key_flat = key_piece.reshape(videos, count_frames * frame_tok, col_count)
    value_flat = value_piece.reshape(videos, count_frames * frame_tok, col_count)
    running = attend(running, key_flat, value_flat, live, query_heads)
    key_piece = lax.all_gather(keys, "seq", axis=1, tiled=True)
    value_piece = lax.all_gather(values, "seq", axis=1, tiled=True)
    length = key_piece.shape[1]
    key_tiles = jnp.arange(length, dtype=jnp.int32) // TILE
    tile_live = jnp.take(tile_mask, key_tiles, axis=2)
    running = attend(
        running, key_piece, value_piece, jnp.repeat(tile_live, TILE, axis=1) > 0, query_heads
    )
    peak, total, summed = running
    result = summed / total[..., None]
    return result.transpose(0, 2, 1, 3).reshape(videos, tok_rows, col_count).astype(jnp.bfloat16)


def head_cols(head):
    start = head * HD
    if not isinstance(head, int):
        start = pl.multiple_of(start, HD)
    return pl.ds(start, HD)


def fill(live):
    return jnp.where(live, 0.0, NEG_FILL)


def frame_fills(place_ref, list_ref, device, frames):
    out = []
    for slot in range(frames):
        held = place_ref[0, device * frames + slot]
        live = held == list_ref[0, 0]
        for entry in range(1, list_ref.shape[1]):
            live = live | (held == list_ref[0, entry])
        out.append(fill(live))
    return out


def rows_of(ref, head):
    if len(ref.shape) == 3:
        return ref[0, :, head_cols(head)]
    return ref[0, :, :, head_cols(head)].reshape(ref.shape[1] * ref.shape[2], HD)


def put(out, row, refs, head):
    for ref in refs:
        block = rows_of(ref, head)
        out[row : row + block.shape[0], :] = block
        row += block.shape[0]
    return row


def pack_kernel(
    half, mask_ref, q_ref, k_ref, v_ref, ck_ref, cv_ref, near0_ref, near1_ref, far2_ref, far3_ref
):
    me = lax.axis_index("seq")
    side = lax.rem(me, 2)
    parts = (q_ref, k_ref, v_ref, ck_ref, cv_ref)
    for rel, out in enumerate((near0_ref, near1_ref, far2_ref, far3_ref)):
        other = jnp.bitwise_xor(me, rel)
        group = (1 - side) if rel % 2 else side
        row = 0
        for j in range(half):
            row = put(out, row, parts if rel < 2 else parts[:1], group * half + j)
        row = put(out, row, parts, 2 * half + other)
        ident = lax.broadcasted_iota(jnp.int32, (FLAG_ROWS, HD), 0)
        block = jnp.zeros((FLAG_ROWS, HD), F32)
        for key in range(4):
            live = mask_ref[0, 0, jnp.bitwise_xor(other, key)] > 0
            block = jnp.where(ident == key, fill(live), block)
        out[row : row + FLAG_ROWS, :] = block.astype(BF16)


def eights(block, reduce):
    return reduce(block.reshape(block.shape[0] // 8, 8, block.shape[1]), axis=0)


def softmax(scores, fills):
    peak = None
    row = 0
    for count, value in fills:
        block = eights(scores[row : row + count, :], jnp.max) * FACTOR + value
        peak = block if peak is None else jnp.maximum(peak, block)
        row += count
    peak = jnp.max(peak, axis=0, keepdims=True)
    weights = []
    total = None
    row = 0
    for count, value in fills:
        block = jnp.exp2(scores[row : row + count, :] * FACTOR - (peak - 2.0 * value))
        part = eights(block, jnp.sum)
        total = part if total is None else total + part
        weights.append(block.astype(BF16))
        row += count
    total = jnp.sum(total, axis=0, keepdims=True)
    total = jnp.where(total == 0.0, 1.0, total)
    return jnp.concatenate(weights, axis=0), 1.0 / total, peak + jnp.log2(total)


def all_fills(refs, keys, frames, frame_tok, list_ref, place_ref, me):
    blocks = []
    for ref in refs:
        row = ref.shape[0] - FLAG_ROWS
        blocks.append(ref[row : row + FLAG_ROWS, :].astype(F32))
    fills = [
        (TILE, jnp.concatenate([block[key : key + 1, :] for block in blocks], axis=1))
        for key in range(keys)
    ]
    for rel in range(keys):
        for value in frame_fills(place_ref, list_ref, jnp.bitwise_xor(me, rel), frames):
            fills.append((frame_tok, value))
    return fills


def stack(places, start, count):
    return jnp.concatenate(
        [ref[base + start : base + start + count, :] for ref, base in places], axis=0
    )


def attend_parts(tasks, cache):
    scores = []
    for query_places, key_places, _ in tasks:
        key_rows = jnp.concatenate(
            [stack(key_places, TILE, TILE), stack(key_places, 3 * TILE, cache)], axis=0
        )
        scores.append(
            lax.dot_general(
                key_rows, stack(query_places, 0, TILE), (((1,), (1,)), ((), ())),
                preferred_element_type=F32,
            )
        )
    softmaxed = [softmax(block, fills) for block, (_, _, fills) in zip(scores, tasks)]
    out = []
    for (weights, scale, logs), (_, key_places, _) in zip(softmaxed, tasks):
        value_rows = jnp.concatenate(
            [stack(key_places, 2 * TILE, TILE), stack(key_places, 3 * TILE + cache, cache)], axis=0
        )
        summed = lax.dot_general(
            value_rows, weights, (((0,), (0,)), ((), ())), preferred_element_type=F32
        )
        out.append((summed * scale, logs))
    return out


def three_parts(row):
    parts = []
    for _ in range(3):
        part = row.astype(BF16).astype(F32)
        parts.append(part)
        row = row - part
    return parts


def stat_block(rows):
    spare = FLAG_ROWS - len(rows)
    return jnp.concatenate(rows + [jnp.zeros((spare, TILE), F32)], axis=0).astype(BF16)


def attend_kernel(
    half, frames, frame_tok,
    list_ref, place_ref, near0_ref, near1_ref, far3_ref, far2_ref,
    own_ref, own_log_ref, whole_ref, out1_ref, out2_ref, out3_ref,
):
    me = lax.axis_index("seq")
    cache = frames * frame_tok
    span = 3 * TILE + 2 * cache
    ins = (near0_ref, near1_ref, far2_ref, far3_ref)
    outs = (out1_ref, out2_ref, out3_ref)
    fills = all_fills(ins, 4, frames, frame_tok, list_ref, place_ref, me)
    pair_fills = fills[:2] + fills[4 : 4 + 2 * frames]
    tasks = []
    for j in range(half):
        pair = ((near0_ref, j * span), (near1_ref, j * span))
        tasks.append((pair + ((far2_ref, j * TILE), (far3_ref, j * TILE)), pair, pair_fills))
    places = [(ref, half * span) for ref in ins[:2]] + [(ref, half * TILE) for ref in ins[2:]]
    tasks.append((places, places, fills))
    *parts, (whole, _) = attend_parts(tasks, cache)
    stats = [[], [], []]
    for j, (summed, logs) in enumerate(parts):
        rows = slice(j * HD, (j + 1) * HD)
        own_ref[rows, :] = summed[:, :TILE]
        own_log_ref[j : j + 1, :] = logs[:, :TILE]
        for rel, out in enumerate(outs, 1):
            cols = slice(rel * TILE, (rel + 1) * TILE)
            out[rows, :] = summed[:, cols].astype(BF16)
            stats[rel - 1] += three_parts(logs[:, cols])
    row = half * HD
    for rel, out in enumerate(outs, 1):
        out[row : row + FLAG_ROWS, :] = stat_block(stats[rel - 1])
        start = row + FLAG_ROWS
        out[start : start + HD, :] = whole[:, rel * TILE : (rel + 1) * TILE].astype(BF16)
    whole_ref[...] = whole[:, :TILE].astype(BF16)


def merge_kernel(
    half, own_ref, own_log_ref, in2_ref, in1_ref, in3_ref,
    whole_ref, out_ref,
):
    me = lax.axis_index("seq")
    side = lax.rem(me, 2)
    start = half * HD

    def logs_of(ref, j):
        block = ref[start : start + FLAG_ROWS, :].astype(F32)
        row = 3 * j
        return block[row : row + 1, :] + block[row + 1 : row + 2, :] + block[row + 2 : row + 3, :]

    def joined(first, first_log, second, second_log):
        peak = jnp.maximum(first_log, second_log)
        first_weight = jnp.exp2(first_log - peak)
        second_weight = jnp.exp2(second_log - peak)
        return (first * first_weight + second * second_weight) / (first_weight + second_weight)

    for j in range(half):
        rows = slice(j * HD, (j + 1) * HD)
        close = joined(
            own_ref[rows, :], own_log_ref[j : j + 1, :],
            in2_ref[rows, :].astype(F32), logs_of(in2_ref, j),
        )
        out_ref[0, :, head_cols(side * half + j)] = close.T.astype(BF16)
        far = joined(
            in1_ref[rows, :].astype(F32), logs_of(in1_ref, j),
            in3_ref[rows, :].astype(F32), logs_of(in3_ref, j),
        )
        out_ref[0, :, head_cols((1 - side) * half + j)] = far.T.astype(BF16)
    done = start + FLAG_ROWS
    blocks = [whole_ref[...]] + [ref[done : done + HD, :] for ref in (in1_ref, in2_ref, in3_ref)]
    for rel, block in enumerate(blocks):
        cols = head_cols(2 * half + jnp.bitwise_xor(me, rel))
        out_ref[0, :, cols] = block.astype(F32).T.astype(BF16)


def send(array, rel):
    return lax.ppermute(array, "seq", [(i, i ^ rel) for i in range(4)])


def near(array):
    return pltpu.with_memory_space_constraint(array, pltpu.VMEM)


def exchanged(queries, keys, values, cache_keys, cache_values, frame_list, frame_place, tile_mask):
    head_count = queries.shape[2] // HD
    half = (head_count - 4) // 2
    frames, frame_tok = cache_keys.shape[1:3]
    span = 3 * TILE + 2 * frames * frame_tok
    pair_rows = (half + 1) * span + FLAG_ROWS
    far_rows = half * TILE + span + FLAG_ROWS
    back_rows = half * HD + FLAG_ROWS
    near0, near1, far2, far3 = pl.pallas_call(
        functools.partial(pack_kernel, half),
        out_shape=(pltpu.VMEM((pair_rows, HD), BF16),) * 2
        + (pltpu.VMEM((far_rows, HD), BF16),) * 2,
        in_specs=[SMEM] + [VMEM] * 5,
        out_specs=(VMEM,) * 4,
    )(tile_mask, queries, keys, values, cache_keys, cache_values)
    near0, near1 = near(near0), near(send(near1, 1))
    far3, far2 = near(send(far3, 3)), near(send(far2, 2))
    own, own_log, whole, back1, back2, back3 = pl.pallas_call(
        functools.partial(attend_kernel, half, frames, frame_tok),
        out_shape=(
            pltpu.VMEM((half * HD, TILE), F32),
            pltpu.VMEM((half, TILE), F32),
            pltpu.VMEM((HD, TILE), BF16),
        ) + (pltpu.VMEM((back_rows + HD, TILE), BF16),) * 3,
        in_specs=[SMEM] * 2 + [VMEM] * 4,
        out_specs=(VMEM,) * 6,
    )(frame_list, frame_place, near0, near1, far3, far2)
    back2, back1, back3 = near(send(back2, 2)), near(send(back1, 1)), near(send(back3, 3))
    return pl.pallas_call(
        functools.partial(merge_kernel, half),
        out_shape=jax.ShapeDtypeStruct(queries.shape, BF16),
        in_specs=[VMEM] * 6,
        out_specs=VMEM,
    )(near(own), near(own_log), back2, back1, back3, near(whole))


def body(queries, keys, values, cache_keys, cache_values, frame_list, frame_place, tile_mask):
    head_count = queries.shape[2] // HD
    fits = (
        lax.axis_size("seq") == 4
        and queries.shape[0] == 1
        and queries.shape[1] == TILE
        and head_count % 2 == 0
        and 6 <= head_count <= 14
    )
    run = exchanged if fits else gathered
    return run(queries, keys, values, cache_keys, cache_values, frame_list, frame_place, tile_mask)


def solution(mesh):
    return jax.shard_map(
        body,
        mesh=mesh,
        in_specs=(
            P(("groups", "batch"), "seq", "head"),
            P(("groups", "batch"), "seq", "head"),
            P(("groups", "batch"), "seq", "head"),
            P(("groups", "batch"), "seq", None, "head"),
            P(("groups", "batch"), "seq", None, "head"),
            P(("groups", "batch"), None),
            P(("groups", "batch"), None),
            P(("groups", "batch"), "seq", None),
        ),
        out_specs=P(("groups", "batch"), "seq", "head"),
        check_vma=False,
    )
```

```python
import functools
import math

import jax
import jax.numpy as jnp
from jax import lax
from jax.experimental import pallas as pl
from jax.experimental.pallas import tpu as pltpu
from jax.sharding import PartitionSpec as P

HD = 128
TILE = 128
NEG_FILL = -1e30
FACTOR = math.log2(math.e) / math.sqrt(HD)
FLAG_ROWS = 16
VMEM = pl.BlockSpec(memory_space=pltpu.VMEM)
SMEM = pl.BlockSpec(memory_space=pltpu.SMEM)
BF16 = jnp.bfloat16
F32 = jnp.float32


def attend(running, key_part, value_part, live, query_heads):
    videos, length, col_count = key_part.shape
    head_count = col_count // HD

    def update(previous):
        peak_old, total_old, summed_old = previous
        key_heads = key_part.reshape(videos, length, head_count, HD)
        value_heads = value_part.reshape(videos, length, head_count, HD)
        scores = jnp.einsum(
            "vqhd,vkhd->vhqk", query_heads, key_heads, preferred_element_type=jnp.float32
        ) * (1.0 / math.sqrt(HD))
        allowed = live[:, None, :, :]
        scores = jnp.where(allowed, scores, NEG_FILL)
        peak_new = jnp.maximum(peak_old, jnp.max(scores, axis=3))
        weights = jnp.where(allowed, jnp.exp(scores - peak_new[..., None]), 0.0)
        factor = jnp.exp(peak_old - peak_new)
        total_new = total_old * factor + jnp.sum(weights, axis=3)
        product = jnp.einsum(
            "vhqk,vkhd->vhqd",
            weights.astype(jnp.bfloat16),
            value_heads,
            preferred_element_type=jnp.float32,
        )
        summed_new = summed_old * factor[..., None] + product
        return (peak_new, total_new, summed_new)

    def unchanged(previous):
        return previous

    return lax.cond(jnp.any(live), update, unchanged, running)


def gathered(queries, keys, values, cache_keys, cache_values, frame_list, frame_place, tile_mask):
    videos, tok_rows, col_count = queries.shape
    head_count = col_count // HD
    query_heads = queries.reshape(videos, tok_rows, head_count, HD)
    running = (
        jnp.full((videos, head_count, tok_rows), NEG_FILL, jnp.float32),
        jnp.zeros((videos, head_count, tok_rows), jnp.float32),
        jnp.zeros((videos, head_count, tok_rows, HD), jnp.float32),
    )
    frame_tok = cache_keys.shape[2]
    listed = jnp.any(frame_place[:, :, None] == frame_list[:, None, :], axis=2)
    key_piece = lax.all_gather(cache_keys, "seq", axis=1, tiled=True)
    value_piece = lax.all_gather(cache_values, "seq", axis=1, tiled=True)
    count_frames = key_piece.shape[1]
    token_flags = jnp.repeat(listed, frame_tok, axis=1)
    live = jnp.broadcast_to(token_flags[:, None, :], (videos, tok_rows, count_frames * frame_tok))
    key_flat = key_piece.reshape(videos, count_frames * frame_tok, col_count)
    value_flat = value_piece.reshape(videos, count_frames * frame_tok, col_count)
    running = attend(running, key_flat, value_flat, live, query_heads)
    key_piece = lax.all_gather(keys, "seq", axis=1, tiled=True)
    value_piece = lax.all_gather(values, "seq", axis=1, tiled=True)
    length = key_piece.shape[1]
    key_tiles = jnp.arange(length, dtype=jnp.int32) // TILE
    tile_live = jnp.take(tile_mask, key_tiles, axis=2)
    running = attend(
        running, key_piece, value_piece, jnp.repeat(tile_live, TILE, axis=1) > 0, query_heads
    )
    peak, total, summed = running
    result = summed / total[..., None]
    return result.transpose(0, 2, 1, 3).reshape(videos, tok_rows, col_count).astype(jnp.bfloat16)


def head_cols(head):
    start = head * HD
    if not isinstance(head, int):
        start = pl.multiple_of(start, HD)
    return pl.ds(start, HD)


def fill(live):
    return jnp.where(live, 0.0, NEG_FILL)


def frame_fills(place_ref, list_ref, me, frames):
    out = []
    for rel in range(4):
        for slot in range(frames):
            held = place_ref[0, jnp.bitwise_xor(me, rel) * frames + slot]
            live = held == list_ref[0, 0]
            for entry in range(1, list_ref.shape[1]):
                live = live | (held == list_ref[0, entry])
            out.append(fill(live))
    return out


def rows_of(ref, head):
    if len(ref.shape) == 3:
        return ref[0, :, head_cols(head)]
    return ref[0, :, :, head_cols(head)].reshape(ref.shape[1] * ref.shape[2], HD)


def put(out, row, refs, head):
    for ref in refs:
        block = rows_of(ref, head)
        out[row : row + block.shape[0], :] = block
        row += block.shape[0]
    return row


def pack_kernel(
    half, rels, mask_ref, list_ref, place_ref, q_ref, k_ref, v_ref, ck_ref, cv_ref, *out_refs
):
    me = lax.axis_index("seq")
    side = lax.rem(me, 2)
    parts = (q_ref, k_ref, v_ref, ck_ref, cv_ref)
    for rel, out in zip(rels, out_refs[-len(rels) :]):
        other = jnp.bitwise_xor(me, rel)
        group = (1 - side) if rel % 2 else side
        row = 0
        for j in range(half):
            row = put(out, row, parts if rel < 2 else parts[:1], group * half + j)
        row = put(out, row, parts, 2 * half + other)
        ident = lax.broadcasted_iota(jnp.int32, (FLAG_ROWS, HD), 0)
        block = jnp.zeros((FLAG_ROWS, HD), F32)
        for key in range(4):
            live = mask_ref[0, 0, jnp.bitwise_xor(other, key)] > 0
            block = jnp.where(ident == key, fill(live), block)
        if rel == 0:
            for key, value in enumerate(frame_fills(place_ref, list_ref, me, ck_ref.shape[1]), 4):
                block = jnp.where(ident == key, value, block)
        out[row : row + FLAG_ROWS, :] = block.astype(BF16)


def eights(block, reduce):
    return reduce(block.reshape(block.shape[0] // 8, 8, block.shape[1]), axis=0)


def softmax(scores, fills):
    peak = None
    row = 0
    for count, value in fills:
        block = eights(scores[row : row + count, :], jnp.max) * FACTOR + value
        peak = block if peak is None else jnp.maximum(peak, block)
        row += count
    peak = jnp.max(peak, axis=0, keepdims=True)
    weights = []
    total = None
    row = 0
    for count, value in fills:
        block = jnp.exp2(scores[row : row + count, :] * FACTOR - (peak - 2.0 * value))
        part = eights(block, jnp.sum)
        total = part if total is None else total + part
        weights.append(block.astype(BF16))
        row += count
    total = jnp.sum(total, axis=0, keepdims=True)
    total = jnp.where(total == 0.0, 1.0, total)
    return jnp.concatenate(weights, axis=0), 1.0 / total, peak + jnp.log2(total)


def all_fills(refs, frames, frame_tok):
    blocks = []
    for ref in refs:
        row = ref.shape[0] - FLAG_ROWS
        blocks.append(ref[row : row + FLAG_ROWS, :].astype(F32))
    fills = [
        (TILE, jnp.concatenate([block[key : key + 1, :] for block in blocks], axis=1))
        for key in range(4)
    ]
    for key in range(4, 4 + 4 * frames):
        row = blocks[0][key : key + 1, :]
        fills.append((frame_tok, jnp.concatenate([row] * 4, axis=1)))
    return fills


def stack(places, start, count):
    return jnp.concatenate(
        [ref[base + start : base + start + count, :] for ref, base in places], axis=0
    )


def attend_parts(tasks, cache):
    scores = []
    for query_places, key_places, _ in tasks:
        key_rows = jnp.concatenate(
            [stack(key_places, TILE, TILE), stack(key_places, 3 * TILE, cache)], axis=0
        )
        scores.append(
            lax.dot_general(
                key_rows, stack(query_places, 0, TILE), (((1,), (1,)), ((), ())),
                preferred_element_type=F32,
            )
        )
    softmaxed = [softmax(block, fills) for block, (_, _, fills) in zip(scores, tasks)]
    out = []
    for (weights, scale, logs), (_, key_places, _) in zip(softmaxed, tasks):
        value_rows = jnp.concatenate(
            [stack(key_places, 2 * TILE, TILE), stack(key_places, 3 * TILE + cache, cache)], axis=0
        )
        summed = lax.dot_general(
            value_rows, weights, (((0,), (0,)), ((), ())), preferred_element_type=F32
        )
        out.append((summed * scale, logs))
    return out


def three_parts(row):
    parts = []
    for _ in range(3):
        part = row.astype(BF16).astype(F32)
        parts.append(part)
        row = row - part
    return parts


def stat_block(rows):
    spare = FLAG_ROWS - len(rows)
    return jnp.concatenate(rows + [jnp.zeros((spare, TILE), F32)], axis=0).astype(BF16)


def attend_kernel(
    half, frames, frame_tok,
    near0_ref, near1_ref, far3_ref, far2_ref,
    own_ref, own_log_ref, whole_ref, out1_ref, out2_ref, out3_ref,
):
    cache = frames * frame_tok
    span = 3 * TILE + 2 * cache
    ins = (near0_ref, near1_ref, far2_ref, far3_ref)
    outs = (out1_ref, out2_ref, out3_ref)
    fills = all_fills(ins, frames, frame_tok)
    pair_fills = fills[:2] + fills[4 : 4 + 2 * frames]
    tasks = []
    for j in range(half):
        pair = ((near0_ref, j * span), (near1_ref, j * span))
        tasks.append((pair + ((far2_ref, j * TILE), (far3_ref, j * TILE)), pair, pair_fills))
    places = [(ref, half * span) for ref in ins[:2]] + [(ref, half * TILE) for ref in ins[2:]]
    tasks.append((places, places, fills))
    *parts, (whole, _) = attend_parts(tasks, cache)
    stats = [[], [], []]
    for j, (summed, logs) in enumerate(parts):
        rows = slice(j * HD, (j + 1) * HD)
        own_ref[rows, :] = summed[:, :TILE]
        own_log_ref[j : j + 1, :] = logs[:, :TILE]
        for rel, out in enumerate(outs, 1):
            cols = slice(rel * TILE, (rel + 1) * TILE)
            out[rows, :] = summed[:, cols].astype(BF16)
            stats[rel - 1] += three_parts(logs[:, cols])
    row = half * HD
    for rel, out in enumerate(outs, 1):
        out[row : row + FLAG_ROWS, :] = stat_block(stats[rel - 1])
        start = row + FLAG_ROWS
        out[start : start + HD, :] = whole[:, rel * TILE : (rel + 1) * TILE].astype(BF16)
    whole_ref[...] = whole[:, :TILE].astype(BF16)


def merge_kernel(
    half, own_ref, own_log_ref, in2_ref, in1_ref, in3_ref,
    whole_ref, out_ref,
):
    me = lax.axis_index("seq")
    side = lax.rem(me, 2)
    start = half * HD

    def logs_of(ref, j):
        block = ref[start : start + FLAG_ROWS, :].astype(F32)
        row = 3 * j
        return block[row : row + 1, :] + block[row + 1 : row + 2, :] + block[row + 2 : row + 3, :]

    def joined(first, first_log, second, second_log):
        peak = jnp.maximum(first_log, second_log)
        first_weight = jnp.exp2(first_log - peak)
        second_weight = jnp.exp2(second_log - peak)
        return (first * first_weight + second * second_weight) / (first_weight + second_weight)

    for j in range(half):
        rows = slice(j * HD, (j + 1) * HD)
        close = joined(
            own_ref[rows, :], own_log_ref[j : j + 1, :],
            in2_ref[rows, :].astype(F32), logs_of(in2_ref, j),
        )
        out_ref[0, :, head_cols(side * half + j)] = close.astype(BF16).T
        far = joined(
            in1_ref[rows, :].astype(F32), logs_of(in1_ref, j),
            in3_ref[rows, :].astype(F32), logs_of(in3_ref, j),
        )
        out_ref[0, :, head_cols((1 - side) * half + j)] = far.astype(BF16).T
    done = start + FLAG_ROWS
    blocks = [whole_ref[...]] + [ref[done : done + HD, :] for ref in (in1_ref, in2_ref, in3_ref)]
    for rel, block in enumerate(blocks):
        cols = head_cols(2 * half + jnp.bitwise_xor(me, rel))
        out_ref[0, :, cols] = block.T


def send(array, rel):
    return lax.ppermute(array, "seq", [(i, i ^ rel) for i in range(4)])


def near(array):
    return pltpu.with_memory_space_constraint(array, pltpu.VMEM)


def exchanged(queries, keys, values, cache_keys, cache_values, frame_list, frame_place, tile_mask):
    head_count = queries.shape[2] // HD
    half = (head_count - 4) // 2
    frames, frame_tok = cache_keys.shape[1:3]
    span = 3 * TILE + 2 * frames * frame_tok
    pair_rows = (half + 1) * span + FLAG_ROWS
    far_rows = half * TILE + span + FLAG_ROWS
    back_rows = half * HD + FLAG_ROWS
    arrays = (tile_mask, frame_list, frame_place, queries, keys, values, cache_keys, cache_values)
    near1 = pl.pallas_call(
        functools.partial(pack_kernel, half, (1,)),
        out_shape=pltpu.VMEM((pair_rows, HD), BF16),
        in_specs=[SMEM] * 3 + [VMEM] * 5,
        out_specs=VMEM,
    )(*arrays)
    far3, far2, near0 = pl.pallas_call(
        functools.partial(pack_kernel, half, (3, 2, 0)),
        out_shape=(pltpu.VMEM((far_rows, HD), BF16),) * 2
        + (pltpu.VMEM((pair_rows, HD), BF16),),
        in_specs=[SMEM] * 3 + [VMEM] * 6,
        out_specs=(VMEM,) * 3,
    )(*arrays, near(near1))
    near0, near1 = near(near0), near(send(near1, 1))
    far3, far2 = near(send(far3, 3)), near(send(far2, 2))
    own, own_log, whole, back1, back2, back3 = pl.pallas_call(
        functools.partial(attend_kernel, half, frames, frame_tok),
        out_shape=(
            pltpu.VMEM((half * HD, TILE), F32),
            pltpu.VMEM((half, TILE), F32),
            pltpu.VMEM((HD, TILE), BF16),
        ) + (pltpu.VMEM((back_rows + HD, TILE), BF16),) * 3,
        in_specs=[VMEM] * 4,
        out_specs=(VMEM,) * 6,
    )(near0, near1, far3, far2)
    back2, back1, back3 = near(send(back2, 2)), near(send(back1, 1)), near(send(back3, 3))
    return pl.pallas_call(
        functools.partial(merge_kernel, half),
        out_shape=jax.ShapeDtypeStruct(queries.shape, BF16),
        in_specs=[VMEM] * 6,
        out_specs=VMEM,
    )(near(own), near(own_log), back2, back1, back3, near(whole))


def body(queries, keys, values, cache_keys, cache_values, frame_list, frame_place, tile_mask):
    head_count = queries.shape[2] // HD
    fits = (
        lax.axis_size("seq") == 4
        and queries.shape[0] == 1
        and queries.shape[1] == TILE
        and head_count % 2 == 0
        and 6 <= head_count <= 14
        and 4 + 4 * cache_keys.shape[1] <= FLAG_ROWS
    )
    run = exchanged if fits else gathered
    return run(queries, keys, values, cache_keys, cache_values, frame_list, frame_place, tile_mask)


def solution(mesh):
    return jax.shard_map(
        body,
        mesh=mesh,
        in_specs=(
            P(("groups", "batch"), "seq", "head"),
            P(("groups", "batch"), "seq", "head"),
            P(("groups", "batch"), "seq", "head"),
            P(("groups", "batch"), "seq", None, "head"),
            P(("groups", "batch"), "seq", None, "head"),
            P(("groups", "batch"), None),
            P(("groups", "batch"), None),
            P(("groups", "batch"), "seq", None),
        ),
        out_specs=P(("groups", "batch"), "seq", "head"),
        check_vma=False,
    )
```

```python
import functools
import math

import jax
import jax.numpy as jnp
from jax import lax
from jax.experimental import pallas as pl
from jax.experimental.pallas import tpu as pltpu
from jax.sharding import PartitionSpec as P

HD = 128
TILE = 128
NEG_FILL = -1e30
FACTOR = math.log2(math.e) / math.sqrt(HD)
FLAG_ROWS = 16
VMEM = pl.BlockSpec(memory_space=pltpu.VMEM)
SMEM = pl.BlockSpec(memory_space=pltpu.SMEM)
BF16 = jnp.bfloat16
F32 = jnp.float32


def attend(running, key_part, value_part, live, query_heads):
    videos, length, col_count = key_part.shape
    head_count = col_count // HD

    def update(previous):
        peak_old, total_old, summed_old = previous
        key_heads = key_part.reshape(videos, length, head_count, HD)
        value_heads = value_part.reshape(videos, length, head_count, HD)
        scores = jnp.einsum(
            "vqhd,vkhd->vhqk", query_heads, key_heads, preferred_element_type=jnp.float32
        ) * (1.0 / math.sqrt(HD))
        allowed = live[:, None, :, :]
        scores = jnp.where(allowed, scores, NEG_FILL)
        peak_new = jnp.maximum(peak_old, jnp.max(scores, axis=3))
        weights = jnp.where(allowed, jnp.exp(scores - peak_new[..., None]), 0.0)
        factor = jnp.exp(peak_old - peak_new)
        total_new = total_old * factor + jnp.sum(weights, axis=3)
        product = jnp.einsum(
            "vhqk,vkhd->vhqd",
            weights.astype(jnp.bfloat16),
            value_heads,
            preferred_element_type=jnp.float32,
        )
        summed_new = summed_old * factor[..., None] + product
        return (peak_new, total_new, summed_new)

    def unchanged(previous):
        return previous

    return lax.cond(jnp.any(live), update, unchanged, running)


def gathered(queries, keys, values, cache_keys, cache_values, frame_list, frame_place, tile_mask):
    videos, tok_rows, col_count = queries.shape
    head_count = col_count // HD
    query_heads = queries.reshape(videos, tok_rows, head_count, HD)
    running = (
        jnp.full((videos, head_count, tok_rows), NEG_FILL, jnp.float32),
        jnp.zeros((videos, head_count, tok_rows), jnp.float32),
        jnp.zeros((videos, head_count, tok_rows, HD), jnp.float32),
    )
    frame_tok = cache_keys.shape[2]
    listed = jnp.any(frame_place[:, :, None] == frame_list[:, None, :], axis=2)
    key_piece = lax.all_gather(cache_keys, "seq", axis=1, tiled=True)
    value_piece = lax.all_gather(cache_values, "seq", axis=1, tiled=True)
    count_frames = key_piece.shape[1]
    token_flags = jnp.repeat(listed, frame_tok, axis=1)
    live = jnp.broadcast_to(token_flags[:, None, :], (videos, tok_rows, count_frames * frame_tok))
    key_flat = key_piece.reshape(videos, count_frames * frame_tok, col_count)
    value_flat = value_piece.reshape(videos, count_frames * frame_tok, col_count)
    running = attend(running, key_flat, value_flat, live, query_heads)
    key_piece = lax.all_gather(keys, "seq", axis=1, tiled=True)
    value_piece = lax.all_gather(values, "seq", axis=1, tiled=True)
    length = key_piece.shape[1]
    key_tiles = jnp.arange(length, dtype=jnp.int32) // TILE
    tile_live = jnp.take(tile_mask, key_tiles, axis=2)
    running = attend(
        running, key_piece, value_piece, jnp.repeat(tile_live, TILE, axis=1) > 0, query_heads
    )
    peak, total, summed = running
    result = summed / total[..., None]
    return result.transpose(0, 2, 1, 3).reshape(videos, tok_rows, col_count).astype(jnp.bfloat16)


def head_cols(head):
    start = head * HD
    if not isinstance(head, int):
        start = pl.multiple_of(start, HD)
    return pl.ds(start, HD)


def fill(live):
    return jnp.where(live, 0.0, NEG_FILL)


def frame_fills(place_ref, list_ref, me, frames):
    out = []
    for rel in range(4):
        for slot in range(frames):
            held = place_ref[0, jnp.bitwise_xor(me, rel) * frames + slot]
            live = held == list_ref[0, 0]
            for entry in range(1, list_ref.shape[1]):
                live = live | (held == list_ref[0, entry])
            out.append(fill(live))
    return out


def rows_of(ref, head):
    if len(ref.shape) == 3:
        return ref[0, :, head_cols(head)]
    return ref[0, :, :, head_cols(head)].reshape(ref.shape[1] * ref.shape[2], HD)


def put(out, row, refs, head):
    for ref in refs:
        block = rows_of(ref, head)
        out[row : row + block.shape[0], :] = block
        row += block.shape[0]
    return row


def pack_kernel(
    half, rels, mask_ref, list_ref, place_ref, q_ref, k_ref, v_ref, ck_ref, cv_ref, *out_refs
):
    me = lax.axis_index("seq")
    side = lax.rem(me, 2)
    parts = (q_ref, k_ref, v_ref, ck_ref, cv_ref)
    for rel, out in zip(rels, out_refs[-len(rels) :]):
        other = jnp.bitwise_xor(me, rel)
        group = (1 - side) if rel % 2 else side
        row = 0
        for j in range(half):
            row = put(out, row, parts if rel < 2 else parts[:1], group * half + j)
        row = put(out, row, parts, 2 * half + other)
        ident = lax.broadcasted_iota(jnp.int32, (FLAG_ROWS, HD), 0)
        block = jnp.zeros((FLAG_ROWS, HD), F32)
        for key in range(4):
            live = mask_ref[0, 0, jnp.bitwise_xor(other, key)] > 0
            block = jnp.where(ident == key, fill(live), block)
        if rel == 0:
            for key, value in enumerate(frame_fills(place_ref, list_ref, me, ck_ref.shape[1]), 4):
                block = jnp.where(ident == key, value, block)
        out[row : row + FLAG_ROWS, :] = block.astype(BF16)


def eights(block, reduce):
    return reduce(block.reshape(block.shape[0] // 8, 8, block.shape[1]), axis=0)


def softmax(scores, fills):
    peak = None
    row = 0
    for count, value in fills:
        block = eights(scores[row : row + count, :], jnp.max) * FACTOR + value
        peak = block if peak is None else jnp.maximum(peak, block)
        row += count
    peak = jnp.max(peak, axis=0, keepdims=True)
    weights = []
    total = None
    row = 0
    for count, value in fills:
        block = jnp.exp2(scores[row : row + count, :] * FACTOR - (peak - 2.0 * value))
        part = eights(block, jnp.sum)
        total = part if total is None else total + part
        weights.append(block.astype(BF16))
        row += count
    total = jnp.sum(total, axis=0, keepdims=True)
    total = jnp.where(total == 0.0, 1.0, total)
    return jnp.concatenate(weights, axis=0), 1.0 / total, peak + jnp.log2(total)


def all_fills(refs, frames, frame_tok):
    blocks = []
    for ref in refs:
        row = ref.shape[0] - FLAG_ROWS
        blocks.append(ref[row : row + FLAG_ROWS, :].astype(F32))
    fills = [
        (TILE, jnp.concatenate([block[key : key + 1, :] for block in blocks], axis=1))
        for key in range(4)
    ]
    for key in range(4, 4 + 4 * frames):
        row = blocks[0][key : key + 1, :]
        fills.append((frame_tok, jnp.concatenate([row] * 4, axis=1)))
    return fills


def stack(places, start, count):
    return jnp.concatenate(
        [ref[base + start : base + start + count, :] for ref, base in places], axis=0
    )


def attend_parts(tasks, cache):
    scores = []
    for query_places, key_places, _ in tasks:
        key_rows = jnp.concatenate(
            [stack(key_places, TILE, TILE), stack(key_places, 3 * TILE, cache)], axis=0
        )
        scores.append(
            lax.dot_general(
                key_rows, stack(query_places, 0, TILE), (((1,), (1,)), ((), ())),
                preferred_element_type=F32,
            )
        )
    softmaxed = [softmax(block, fills) for block, (_, _, fills) in zip(scores, tasks)]
    out = []
    for (weights, scale, logs), (_, key_places, _) in zip(softmaxed, tasks):
        value_rows = jnp.concatenate(
            [stack(key_places, 2 * TILE, TILE), stack(key_places, 3 * TILE + cache, cache)], axis=0
        )
        summed = lax.dot_general(
            value_rows, weights, (((0,), (0,)), ((), ())), preferred_element_type=F32
        )
        out.append((summed * scale, logs))
    return out


def three_parts(row):
    parts = []
    for _ in range(3):
        part = row.astype(BF16).astype(F32)
        parts.append(part)
        row = row - part
    return parts


def stat_block(rows):
    spare = FLAG_ROWS - len(rows)
    return jnp.concatenate(rows + [jnp.zeros((spare, TILE), F32)], axis=0).astype(BF16)


def attend_kernel(
    half, frames, frame_tok,
    near0_ref, near1_ref, far3_ref, far2_ref,
    own_ref, own_log_ref, whole_ref, out1_ref, out2_ref, out3_ref,
):
    cache = frames * frame_tok
    span = 3 * TILE + 2 * cache
    ins = (near0_ref, near1_ref, far2_ref, far3_ref)
    outs = (out1_ref, out2_ref, out3_ref)
    fills = all_fills(ins, frames, frame_tok)
    pair_fills = fills[:2] + fills[4 : 4 + 2 * frames]
    tasks = []
    for j in range(half):
        pair = ((near0_ref, j * span), (near1_ref, j * span))
        tasks.append((pair + ((far2_ref, j * TILE), (far3_ref, j * TILE)), pair, pair_fills))
    places = [(ref, half * span) for ref in ins[:2]] + [(ref, half * TILE) for ref in ins[2:]]
    tasks.append((places, places, fills))
    *parts, (whole, _) = attend_parts(tasks, cache)
    stats = [[], [], []]
    for j, (summed, logs) in enumerate(parts):
        rows = slice(j * HD, (j + 1) * HD)
        own_ref[rows, :] = summed[:, :TILE]
        own_log_ref[j : j + 1, :] = logs[:, :TILE]
        for rel, out in enumerate(outs, 1):
            cols = slice(rel * TILE, (rel + 1) * TILE)
            out[rows, :] = summed[:, cols].astype(BF16)
            stats[rel - 1] += three_parts(logs[:, cols])
    row = half * HD
    for rel, out in enumerate(outs, 1):
        out[row : row + FLAG_ROWS, :] = stat_block(stats[rel - 1])
        start = row + FLAG_ROWS
        out[start : start + HD, :] = whole[:, rel * TILE : (rel + 1) * TILE].astype(BF16)
    whole_ref[...] = whole[:, :TILE].astype(BF16)


def merge_kernel(
    half, own_ref, own_log_ref, in2_ref, in1_ref, in3_ref,
    whole_ref, out_hbm, out_ref, sems,
):
    me = lax.axis_index("seq")
    side = lax.rem(me, 2)
    start = half * HD

    def logs_of(ref, j):
        block = ref[start : start + FLAG_ROWS, :].astype(F32)
        row = 3 * j
        return block[row : row + 1, :] + block[row + 1 : row + 2, :] + block[row + 2 : row + 3, :]

    def joined(first, first_log, second, second_log):
        peak = jnp.maximum(first_log, second_log)
        first_weight = jnp.exp2(first_log - peak)
        second_weight = jnp.exp2(second_log - peak)
        scale = 1.0 / (first_weight + second_weight)
        return first * (first_weight * scale) + second * (second_weight * scale)

    copies = []

    def leave(head, count):
        cols = pl.ds(pl.multiple_of(head * HD, HD), count * HD)
        copy = pltpu.make_async_copy(
            out_ref.at[0, :, cols], out_hbm.at[0, :, cols], sems.at[len(copies)]
        )
        copy.start()
        copies.append(copy)

    done = start + FLAG_ROWS
    blocks = [whole_ref[...]] + [ref[done : done + HD, :] for ref in (in1_ref, in2_ref, in3_ref)]
    for rel, block in enumerate(blocks):
        cols = head_cols(2 * half + jnp.bitwise_xor(me, rel))
        out_ref[0, :, cols] = block.T
    leave(2 * half, 4)
    for j in range(half):
        rows = slice(j * HD, (j + 1) * HD)
        far = joined(
            in1_ref[rows, :].astype(F32), logs_of(in1_ref, j),
            in3_ref[rows, :].astype(F32), logs_of(in3_ref, j),
        )
        out_ref[0, :, head_cols((1 - side) * half + j)] = far.astype(BF16).T
    leave((1 - side) * half, half)
    for j in range(half):
        rows = slice(j * HD, (j + 1) * HD)
        close = joined(
            own_ref[rows, :], own_log_ref[j : j + 1, :],
            in2_ref[rows, :].astype(F32), logs_of(in2_ref, j),
        )
        out_ref[0, :, head_cols(side * half + j)] = close.astype(BF16).T
    leave(side * half, half)
    for copy in copies:
        copy.wait()


def send(array, rel):
    return lax.ppermute(array, "seq", [(i, i ^ rel) for i in range(4)])


def near(array):
    return pltpu.with_memory_space_constraint(array, pltpu.VMEM)


def exchanged(queries, keys, values, cache_keys, cache_values, frame_list, frame_place, tile_mask):
    head_count = queries.shape[2] // HD
    half = (head_count - 4) // 2
    frames, frame_tok = cache_keys.shape[1:3]
    span = 3 * TILE + 2 * frames * frame_tok
    pair_rows = (half + 1) * span + FLAG_ROWS
    far_rows = half * TILE + span + FLAG_ROWS
    back_rows = half * HD + FLAG_ROWS
    arrays = (tile_mask, frame_list, frame_place, queries, keys, values, cache_keys, cache_values)
    near1, far3, far2 = pl.pallas_call(
        functools.partial(pack_kernel, half, (1, 3, 2)),
        out_shape=(pltpu.VMEM((pair_rows, HD), BF16),)
        + (pltpu.VMEM((far_rows, HD), BF16),) * 2,
        in_specs=[SMEM] * 3 + [VMEM] * 5,
        out_specs=(VMEM,) * 3,
    )(*arrays)
    near0 = pl.pallas_call(
        functools.partial(pack_kernel, half, (0,)),
        out_shape=pltpu.VMEM((pair_rows, HD), BF16),
        in_specs=[SMEM] * 3 + [VMEM] * 6,
        out_specs=VMEM,
    )(*arrays, near(far2))
    near0, near1 = near(near0), near(send(near1, 1))
    far3, far2 = near(send(far3, 3)), near(send(far2, 2))
    own, own_log, whole, back1, back2, back3 = pl.pallas_call(
        functools.partial(attend_kernel, half, frames, frame_tok),
        out_shape=(
            pltpu.VMEM((half * HD, TILE), F32),
            pltpu.VMEM((half, TILE), F32),
            pltpu.VMEM((HD, TILE), BF16),
        ) + (pltpu.VMEM((back_rows + HD, TILE), BF16),) * 3,
        in_specs=[VMEM] * 4,
        out_specs=(VMEM,) * 6,
    )(near0, near1, far3, far2)
    back2, back1, back3 = near(send(back2, 2)), near(send(back1, 1)), near(send(back3, 3))
    return pl.pallas_call(
        functools.partial(merge_kernel, half),
        out_shape=jax.ShapeDtypeStruct(queries.shape, BF16),
        in_specs=[VMEM] * 6,
        out_specs=pl.BlockSpec(memory_space=pl.ANY),
        scratch_shapes=[pltpu.VMEM(queries.shape, BF16), pltpu.SemaphoreType.DMA((3,))],
    )(near(own), near(own_log), back2, back1, back3, near(whole))


def body(queries, keys, values, cache_keys, cache_values, frame_list, frame_place, tile_mask):
    head_count = queries.shape[2] // HD
    fits = (
        lax.axis_size("seq") == 4
        and queries.shape[0] == 1
        and queries.shape[1] == TILE
        and head_count % 2 == 0
        and 6 <= head_count <= 14
        and 4 + 4 * cache_keys.shape[1] <= FLAG_ROWS
    )
    run = exchanged if fits else gathered
    return run(queries, keys, values, cache_keys, cache_values, frame_list, frame_place, tile_mask)


def solution(mesh):
    return jax.shard_map(
        body,
        mesh=mesh,
        in_specs=(
            P(("groups", "batch"), "seq", "head"),
            P(("groups", "batch"), "seq", "head"),
            P(("groups", "batch"), "seq", "head"),
            P(("groups", "batch"), "seq", None, "head"),
            P(("groups", "batch"), "seq", None, "head"),
            P(("groups", "batch"), None),
            P(("groups", "batch"), None),
            P(("groups", "batch"), "seq", None),
        ),
        out_specs=P(("groups", "batch"), "seq", "head"),
        check_vma=False,
    )
```

```python
import functools
import math

import jax
import jax.numpy as jnp
from jax import lax
from jax.experimental import pallas as pl
from jax.experimental.pallas import tpu as pltpu
from jax.sharding import PartitionSpec as P

HD = 128
TILE = 128
NEG_FILL = -1e30
FACTOR = math.log2(math.e) / math.sqrt(HD)
FLAG_ROWS = 16
VMEM = pl.BlockSpec(memory_space=pltpu.VMEM)
SMEM = pl.BlockSpec(memory_space=pltpu.SMEM)
BF16 = jnp.bfloat16
F32 = jnp.float32


def attend(running, key_part, value_part, live, query_heads):
    videos, length, col_count = key_part.shape
    head_count = col_count // HD

    def update(previous):
        peak_old, total_old, summed_old = previous
        key_heads = key_part.reshape(videos, length, head_count, HD)
        value_heads = value_part.reshape(videos, length, head_count, HD)
        scores = jnp.einsum(
            "vqhd,vkhd->vhqk", query_heads, key_heads, preferred_element_type=jnp.float32
        ) * (1.0 / math.sqrt(HD))
        allowed = live[:, None, :, :]
        scores = jnp.where(allowed, scores, NEG_FILL)
        peak_new = jnp.maximum(peak_old, jnp.max(scores, axis=3))
        weights = jnp.where(allowed, jnp.exp(scores - peak_new[..., None]), 0.0)
        factor = jnp.exp(peak_old - peak_new)
        total_new = total_old * factor + jnp.sum(weights, axis=3)
        product = jnp.einsum(
            "vhqk,vkhd->vhqd",
            weights.astype(jnp.bfloat16),
            value_heads,
            preferred_element_type=jnp.float32,
        )
        summed_new = summed_old * factor[..., None] + product
        return (peak_new, total_new, summed_new)

    def unchanged(previous):
        return previous

    return lax.cond(jnp.any(live), update, unchanged, running)


def gathered(queries, keys, values, cache_keys, cache_values, frame_list, frame_place, tile_mask):
    videos, tok_rows, col_count = queries.shape
    head_count = col_count // HD
    query_heads = queries.reshape(videos, tok_rows, head_count, HD)
    running = (
        jnp.full((videos, head_count, tok_rows), NEG_FILL, jnp.float32),
        jnp.zeros((videos, head_count, tok_rows), jnp.float32),
        jnp.zeros((videos, head_count, tok_rows, HD), jnp.float32),
    )
    frame_tok = cache_keys.shape[2]
    listed = jnp.any(frame_place[:, :, None] == frame_list[:, None, :], axis=2)
    key_piece = lax.all_gather(cache_keys, "seq", axis=1, tiled=True)
    value_piece = lax.all_gather(cache_values, "seq", axis=1, tiled=True)
    count_frames = key_piece.shape[1]
    token_flags = jnp.repeat(listed, frame_tok, axis=1)
    live = jnp.broadcast_to(token_flags[:, None, :], (videos, tok_rows, count_frames * frame_tok))
    key_flat = key_piece.reshape(videos, count_frames * frame_tok, col_count)
    value_flat = value_piece.reshape(videos, count_frames * frame_tok, col_count)
    running = attend(running, key_flat, value_flat, live, query_heads)
    key_piece = lax.all_gather(keys, "seq", axis=1, tiled=True)
    value_piece = lax.all_gather(values, "seq", axis=1, tiled=True)
    length = key_piece.shape[1]
    key_tiles = jnp.arange(length, dtype=jnp.int32) // TILE
    tile_live = jnp.take(tile_mask, key_tiles, axis=2)
    running = attend(
        running, key_piece, value_piece, jnp.repeat(tile_live, TILE, axis=1) > 0, query_heads
    )
    peak, total, summed = running
    result = summed / total[..., None]
    return result.transpose(0, 2, 1, 3).reshape(videos, tok_rows, col_count).astype(jnp.bfloat16)


def head_cols(head):
    start = head * HD
    if not isinstance(head, int):
        start = pl.multiple_of(start, HD)
    return pl.ds(start, HD)


def fill(live):
    return jnp.where(live, 0.0, NEG_FILL)


def frame_fills(place_ref, list_ref, me, frames):
    out = []
    for rel in range(4):
        for slot in range(frames):
            held = place_ref[0, jnp.bitwise_xor(me, rel) * frames + slot]
            live = held == list_ref[0, 0]
            for entry in range(1, list_ref.shape[1]):
                live = live | (held == list_ref[0, entry])
            out.append(fill(live))
    return out


def rows_of(ref, head):
    if len(ref.shape) == 3:
        return ref[0, :, head_cols(head)]
    return ref[0, :, :, head_cols(head)].reshape(ref.shape[1] * ref.shape[2], HD)


def put(out, row, refs, head):
    for ref in refs:
        block = rows_of(ref, head)
        out[row : row + block.shape[0], :] = block
        row += block.shape[0]
    return row


def pack_copies(half, rel, me, parts, out):
    side = lax.rem(me, 2)
    group = (1 - side) if rel % 2 else side
    heads = [group * half + j for j in range(half)] + [2 * half + jnp.bitwise_xor(me, rel)]
    views = []
    row = 0
    for j, head in enumerate(heads):
        for part in parts if rel < 2 or j == half else parts[:1]:
            pieces = [(0,)] if len(part.shape) == 3 else [(0, i) for i in range(part.shape[1])]
            for piece in pieces:
                count = part.shape[-2]
                source = part.at[(*piece, slice(None), head_cols(head))]
                views.append((source, out.at[pl.ds(row, count), :]))
                row += count
    return views


def pack_kernel(half, rels, *refs):
    scalars, parts = refs[:3], refs[3:8]
    mask_ref, list_ref, place_ref, sems = refs[-4:]
    out_refs = refs[-4 - len(rels) : -4]
    me = lax.axis_index("seq")
    views = list(zip(scalars, (mask_ref, list_ref, place_ref)))[: 3 if 0 in rels else 1]
    used = len(views)
    for rel, out in zip(rels, out_refs):
        views += pack_copies(half, rel, me, parts, out)
    copies = [
        pltpu.make_async_copy(source, target, sems.at[i])
        for i, (source, target) in enumerate(views)
    ]
    for copy in copies:
        copy.start()
    for copy in copies[:used]:
        copy.wait()
    for rel, out in zip(rels, out_refs):
        other = jnp.bitwise_xor(me, rel)
        ident = lax.broadcasted_iota(jnp.int32, (FLAG_ROWS, HD), 0)
        block = jnp.zeros((FLAG_ROWS, HD), F32)
        for key in range(4):
            live = mask_ref[0, 0, jnp.bitwise_xor(other, key)] > 0
            block = jnp.where(ident == key, fill(live), block)
        if rel == 0:
            frames = parts[3].shape[1]
            for key, value in enumerate(frame_fills(place_ref, list_ref, me, frames), 4):
                block = jnp.where(ident == key, value, block)
        row = out.shape[0] - FLAG_ROWS
        out[row : row + FLAG_ROWS, :] = block.astype(BF16)
    for copy in copies[used:]:
        copy.wait()


def eights(block, reduce):
    return reduce(block.reshape(block.shape[0] // 8, 8, block.shape[1]), axis=0)


def softmax(scores, fills):
    peak = None
    row = 0
    for count, value in fills:
        block = eights(scores[row : row + count, :], jnp.max) * FACTOR + value
        peak = block if peak is None else jnp.maximum(peak, block)
        row += count
    peak = jnp.max(peak, axis=0, keepdims=True)
    weights = []
    total = None
    row = 0
    for count, value in fills:
        block = jnp.exp2(scores[row : row + count, :] * FACTOR - (peak - 2.0 * value))
        part = eights(block, jnp.sum)
        total = part if total is None else total + part
        weights.append(block.astype(BF16))
        row += count
    total = jnp.sum(total, axis=0, keepdims=True)
    total = jnp.where(total == 0.0, 1.0, total)
    return jnp.concatenate(weights, axis=0), 1.0 / total, peak + jnp.log2(total)


def all_fills(refs, frames, frame_tok):
    blocks = []
    for ref in refs:
        row = ref.shape[0] - FLAG_ROWS
        blocks.append(ref[row : row + FLAG_ROWS, :].astype(F32))
    fills = [
        (TILE, jnp.concatenate([block[key : key + 1, :] for block in blocks], axis=1))
        for key in range(4)
    ]
    for key in range(4, 4 + 4 * frames):
        row = blocks[0][key : key + 1, :]
        fills.append((frame_tok, jnp.concatenate([row] * len(refs), axis=1)))
    return fills


def stack(places, start, count):
    return jnp.concatenate(
        [ref[base + start : base + start + count, :] for ref, base in places], axis=0
    )


def attend_parts(tasks, cache):
    scores = []
    for query_places, key_places, _ in tasks:
        key_rows = jnp.concatenate(
            [stack(key_places, TILE, TILE), stack(key_places, 3 * TILE, cache)], axis=0
        )
        scores.append(
            lax.dot_general(
                key_rows, stack(query_places, 0, TILE), (((1,), (1,)), ((), ())),
                preferred_element_type=F32,
            )
        )
    softmaxed = [softmax(block, fills) for block, (_, _, fills) in zip(scores, tasks)]
    out = []
    for (weights, scale, logs), (_, key_places, _) in zip(softmaxed, tasks):
        value_rows = jnp.concatenate(
            [stack(key_places, 2 * TILE, TILE), stack(key_places, 3 * TILE + cache, cache)], axis=0
        )
        summed = lax.dot_general(
            value_rows, weights, (((0,), (0,)), ((), ())), preferred_element_type=F32
        )
        out.append((summed * scale, logs))
    return out


def three_parts(row):
    parts = []
    for _ in range(3):
        part = row.astype(BF16).astype(F32)
        parts.append(part)
        row = row - part
    return parts


def stat_block(rows):
    spare = FLAG_ROWS - len(rows)
    return jnp.concatenate(rows + [jnp.zeros((spare, TILE), F32)], axis=0).astype(BF16)


def early_kernel(
    half, frames, frame_tok, near0_ref, near1_ref, far3_ref,
    own_ref, own_log_ref, out1_ref, out3_ref,
):
    cache = frames * frame_tok
    span = 3 * TILE + 2 * cache
    fills = all_fills((near0_ref, near1_ref, far3_ref), frames, frame_tok)
    fills = fills[:2] + fills[4 : 4 + 2 * frames]
    tasks = []
    for j in range(half):
        pair = ((near0_ref, j * span), (near1_ref, j * span))
        tasks.append((pair + ((far3_ref, j * TILE),), pair, fills))
    stats = [[], []]
    outs = (out1_ref, out3_ref)
    for j, (summed, logs) in enumerate(attend_parts(tasks, cache)):
        rows = slice(j * HD, (j + 1) * HD)
        own_ref[rows, :] = summed[:, :TILE]
        own_log_ref[j : j + 1, :] = logs[:, :TILE]
        for i, out in enumerate(outs):
            cols = slice((i + 1) * TILE, (i + 2) * TILE)
            out[rows, :] = summed[:, cols].astype(BF16)
            stats[i] += three_parts(logs[:, cols])
    for i, out in enumerate(outs):
        out[half * HD : half * HD + FLAG_ROWS, :] = stat_block(stats[i])


def late_kernel(
    half, frames, frame_tok, near0_ref, near1_ref, far3_ref, far2_ref, early1_ref, early3_ref,
    whole_ref, out1_ref, out2_ref, out3_ref,
):
    cache = frames * frame_tok
    span = 3 * TILE + 2 * cache
    ins = (near0_ref, near1_ref, far2_ref, far3_ref)
    fills = all_fills(ins, frames, frame_tok)
    cols = slice(2 * TILE, 3 * TILE)
    pair_fills = [
        (count, value[:, cols]) for count, value in fills[:2] + fills[4 : 4 + 2 * frames]
    ]
    tasks = []
    for j in range(half):
        pair = ((near0_ref, j * span), (near1_ref, j * span))
        tasks.append((((far2_ref, j * TILE),), pair, pair_fills))
    places = [(ref, half * span) for ref in ins[:2]] + [(ref, half * TILE) for ref in ins[2:]]
    tasks.append((places, places, fills))
    *parts, (whole, _) = attend_parts(tasks, cache)
    stats = []
    for j, (summed, logs) in enumerate(parts):
        out2_ref[j * HD : (j + 1) * HD, :] = summed.astype(BF16)
        stats += three_parts(logs)
    row = half * HD
    start = row + FLAG_ROWS
    out2_ref[row:start, :] = stat_block(stats)
    out1_ref[0:start, :] = early1_ref[...]
    out3_ref[0:start, :] = early3_ref[...]
    whole_ref[...] = whole[:, :TILE].astype(BF16)
    for rel, out in enumerate((out1_ref, out2_ref, out3_ref), 1):
        out[start : start + HD, :] = whole[:, rel * TILE : (rel + 1) * TILE].astype(BF16)


def merge_kernel(
    half, own_ref, own_log_ref, in2_ref, in1_ref, in3_ref,
    whole_ref, out_hbm, out_ref, sems,
):
    me = lax.axis_index("seq")
    side = lax.rem(me, 2)
    start = half * HD

    def logs_of(ref, j):
        block = ref[start : start + FLAG_ROWS, :].astype(F32)
        row = 3 * j
        return block[row : row + 1, :] + block[row + 1 : row + 2, :] + block[row + 2 : row + 3, :]

    def joined(first, first_log, second, second_log):
        peak = jnp.maximum(first_log, second_log)
        first_weight = jnp.exp2(first_log - peak)
        second_weight = jnp.exp2(second_log - peak)
        scale = 1.0 / (first_weight + second_weight)
        return first * (first_weight * scale) + second * (second_weight * scale)

    copies = []

    def leave(head, count):
        cols = pl.ds(pl.multiple_of(head * HD, HD), count * HD)
        copy = pltpu.make_async_copy(
            out_ref.at[0, :, cols], out_hbm.at[0, :, cols], sems.at[len(copies)]
        )
        copy.start()
        copies.append(copy)

    done = start + FLAG_ROWS
    blocks = [whole_ref[...]] + [ref[done : done + HD, :] for ref in (in1_ref, in2_ref, in3_ref)]
    for rel, block in enumerate(blocks):
        cols = head_cols(2 * half + jnp.bitwise_xor(me, rel))
        out_ref[0, :, cols] = block.T
    leave(2 * half, 4)
    for j in range(half):
        rows = slice(j * HD, (j + 1) * HD)
        far = joined(
            in1_ref[rows, :].astype(F32), logs_of(in1_ref, j),
            in3_ref[rows, :].astype(F32), logs_of(in3_ref, j),
        )
        out_ref[0, :, head_cols((1 - side) * half + j)] = far.astype(BF16).T
    leave((1 - side) * half, half)
    for j in range(half):
        rows = slice(j * HD, (j + 1) * HD)
        close = joined(
            own_ref[rows, :], own_log_ref[j : j + 1, :],
            in2_ref[rows, :].astype(F32), logs_of(in2_ref, j),
        )
        out_ref[0, :, head_cols(side * half + j)] = close.astype(BF16).T
    leave(side * half, half)
    for copy in copies:
        copy.wait()


def send(array, rel):
    return lax.ppermute(array, "seq", [(i, i ^ rel) for i in range(4)])


def near(array):
    return pltpu.with_memory_space_constraint(array, pltpu.VMEM)


def exchanged(queries, keys, values, cache_keys, cache_values, frame_list, frame_place, tile_mask):
    head_count = queries.shape[2] // HD
    half = (head_count - 4) // 2
    frames, frame_tok = cache_keys.shape[1:3]
    span = 3 * TILE + 2 * frames * frame_tok
    pair_rows = (half + 1) * span + FLAG_ROWS
    far_rows = half * TILE + span + FLAG_ROWS
    back_rows = half * HD + FLAG_ROWS
    scalars = [pltpu.SMEM(array.shape, jnp.int32) for array in (tile_mask, frame_list, frame_place)]
    once = [pl.BlockSpec(memory_space=pl.ANY)]
    arrays = (tile_mask, frame_list, frame_place, queries, keys, values, cache_keys, cache_values)
    near1 = pl.pallas_call(
        functools.partial(pack_kernel, half, (1,)),
        out_shape=pltpu.VMEM((pair_rows, HD), BF16),
        in_specs=once * 8,
        out_specs=VMEM,
        scratch_shapes=scalars + [pltpu.SemaphoreType.DMA((3 + (half + 1) * (3 + 2 * frames),))],
    )(*arrays)
    far3, far2 = pl.pallas_call(
        functools.partial(pack_kernel, half, (3, 2)),
        out_shape=(pltpu.VMEM((far_rows, HD), BF16),) * 2,
        in_specs=once * 9,
        out_specs=(VMEM,) * 2,
        scratch_shapes=scalars + [pltpu.SemaphoreType.DMA((3 + 2 * (half + 3 + 2 * frames),))],
    )(*arrays, near(near1))
    near0 = pl.pallas_call(
        functools.partial(pack_kernel, half, (0,)),
        out_shape=pltpu.VMEM((pair_rows, HD), BF16),
        in_specs=once * 9,
        out_specs=VMEM,
        scratch_shapes=scalars + [pltpu.SemaphoreType.DMA((3 + (half + 1) * (3 + 2 * frames),))],
    )(*arrays, near(far2))
    near0, near1 = near(near0), near(send(near1, 1))
    far3, far2 = near(send(far3, 3)), near(send(far2, 2))
    own, own_log, early1, early3 = pl.pallas_call(
        functools.partial(early_kernel, half, frames, frame_tok),
        out_shape=(
            pltpu.VMEM((half * HD, TILE), F32),
            pltpu.VMEM((half, TILE), F32),
        ) + (pltpu.VMEM((back_rows, TILE), BF16),) * 2,
        in_specs=[VMEM] * 3,
        out_specs=(VMEM,) * 4,
    )(near0, near1, far3)
    whole, back1, back2, back3 = pl.pallas_call(
        functools.partial(late_kernel, half, frames, frame_tok),
        out_shape=(pltpu.VMEM((HD, TILE), BF16),)
        + (pltpu.VMEM((back_rows + HD, TILE), BF16),) * 3,
        in_specs=[VMEM] * 6,
        out_specs=(VMEM,) * 4,
    )(near0, near1, far3, far2, near(early1), near(early3))
    back2, back1, back3 = near(send(back2, 2)), near(send(back1, 1)), near(send(back3, 3))
    return pl.pallas_call(
        functools.partial(merge_kernel, half),
        out_shape=jax.ShapeDtypeStruct(queries.shape, BF16),
        in_specs=[VMEM] * 6,
        out_specs=pl.BlockSpec(memory_space=pl.ANY),
        scratch_shapes=[pltpu.VMEM(queries.shape, BF16), pltpu.SemaphoreType.DMA((3,))],
    )(near(own), near(own_log), back2, back1, back3, near(whole))


def body(queries, keys, values, cache_keys, cache_values, frame_list, frame_place, tile_mask):
    head_count = queries.shape[2] // HD
    fits = (
        lax.axis_size("seq") == 4
        and queries.shape[0] == 1
        and queries.shape[1] == TILE
        and head_count % 2 == 0
        and 6 <= head_count <= 14
        and 4 + 4 * cache_keys.shape[1] <= FLAG_ROWS
    )
    run = exchanged if fits else gathered
    return run(queries, keys, values, cache_keys, cache_values, frame_list, frame_place, tile_mask)


def solution(mesh):
    return jax.shard_map(
        body,
        mesh=mesh,
        in_specs=(
            P(("groups", "batch"), "seq", "head"),
            P(("groups", "batch"), "seq", "head"),
            P(("groups", "batch"), "seq", "head"),
            P(("groups", "batch"), "seq", None, "head"),
            P(("groups", "batch"), "seq", None, "head"),
            P(("groups", "batch"), None),
            P(("groups", "batch"), None),
            P(("groups", "batch"), "seq", None),
        ),
        out_specs=P(("groups", "batch"), "seq", "head"),
        check_vma=False,
    )
```

```python
import functools
import math

import jax
import jax.numpy as jnp
from jax import lax
from jax.experimental import pallas as pl
from jax.experimental.pallas import tpu as pltpu
from jax.sharding import PartitionSpec as P

HD = 128
TILE = 128
NEG_FILL = -1e30
FACTOR = math.log2(math.e) / math.sqrt(HD)
FLAG_ROWS = 16
VMEM = pl.BlockSpec(memory_space=pltpu.VMEM)
SMEM = pl.BlockSpec(memory_space=pltpu.SMEM)
BF16 = jnp.bfloat16
F32 = jnp.float32


def attend(running, key_part, value_part, live, query_heads):
    videos, length, col_count = key_part.shape
    head_count = col_count // HD

    def update(previous):
        peak_old, total_old, summed_old = previous
        key_heads = key_part.reshape(videos, length, head_count, HD)
        value_heads = value_part.reshape(videos, length, head_count, HD)
        scores = jnp.einsum(
            "vqhd,vkhd->vhqk", query_heads, key_heads, preferred_element_type=jnp.float32
        ) * (1.0 / math.sqrt(HD))
        allowed = live[:, None, :, :]
        scores = jnp.where(allowed, scores, NEG_FILL)
        peak_new = jnp.maximum(peak_old, jnp.max(scores, axis=3))
        weights = jnp.where(allowed, jnp.exp(scores - peak_new[..., None]), 0.0)
        factor = jnp.exp(peak_old - peak_new)
        total_new = total_old * factor + jnp.sum(weights, axis=3)
        product = jnp.einsum(
            "vhqk,vkhd->vhqd",
            weights.astype(jnp.bfloat16),
            value_heads,
            preferred_element_type=jnp.float32,
        )
        summed_new = summed_old * factor[..., None] + product
        return (peak_new, total_new, summed_new)

    def unchanged(previous):
        return previous

    return lax.cond(jnp.any(live), update, unchanged, running)


def gathered(queries, keys, values, cache_keys, cache_values, frame_list, frame_place, tile_mask):
    videos, tok_rows, col_count = queries.shape
    head_count = col_count // HD
    query_heads = queries.reshape(videos, tok_rows, head_count, HD)
    running = (
        jnp.full((videos, head_count, tok_rows), NEG_FILL, jnp.float32),
        jnp.zeros((videos, head_count, tok_rows), jnp.float32),
        jnp.zeros((videos, head_count, tok_rows, HD), jnp.float32),
    )
    frame_tok = cache_keys.shape[2]
    listed = jnp.any(frame_place[:, :, None] == frame_list[:, None, :], axis=2)
    key_piece = lax.all_gather(cache_keys, "seq", axis=1, tiled=True)
    value_piece = lax.all_gather(cache_values, "seq", axis=1, tiled=True)
    count_frames = key_piece.shape[1]
    token_flags = jnp.repeat(listed, frame_tok, axis=1)
    live = jnp.broadcast_to(token_flags[:, None, :], (videos, tok_rows, count_frames * frame_tok))
    key_flat = key_piece.reshape(videos, count_frames * frame_tok, col_count)
    value_flat = value_piece.reshape(videos, count_frames * frame_tok, col_count)
    running = attend(running, key_flat, value_flat, live, query_heads)
    key_piece = lax.all_gather(keys, "seq", axis=1, tiled=True)
    value_piece = lax.all_gather(values, "seq", axis=1, tiled=True)
    length = key_piece.shape[1]
    key_tiles = jnp.arange(length, dtype=jnp.int32) // TILE
    tile_live = jnp.take(tile_mask, key_tiles, axis=2)
    running = attend(
        running, key_piece, value_piece, jnp.repeat(tile_live, TILE, axis=1) > 0, query_heads
    )
    peak, total, summed = running
    result = summed / total[..., None]
    return result.transpose(0, 2, 1, 3).reshape(videos, tok_rows, col_count).astype(jnp.bfloat16)


def head_cols(head):
    start = head * HD
    if not isinstance(head, int):
        start = pl.multiple_of(start, HD)
    return pl.ds(start, HD)


def fill(live):
    return jnp.where(live, 0.0, NEG_FILL)


def frame_fills(place_ref, list_ref, me, frames):
    out = []
    for rel in range(4):
        for slot in range(frames):
            held = place_ref[0, jnp.bitwise_xor(me, rel) * frames + slot]
            live = held == list_ref[0, 0]
            for entry in range(1, list_ref.shape[1]):
                live = live | (held == list_ref[0, entry])
            out.append(fill(live))
    return out


def rows_of(ref, head):
    if len(ref.shape) == 3:
        return ref[0, :, head_cols(head)]
    return ref[0, :, :, head_cols(head)].reshape(ref.shape[1] * ref.shape[2], HD)


def put(out, row, refs, head):
    for ref in refs:
        block = rows_of(ref, head)
        out[row : row + block.shape[0], :] = block
        row += block.shape[0]
    return row


def pack_copies(half, rel, me, parts, out):
    side = lax.rem(me, 2)
    group = (1 - side) if rel % 2 else side
    heads = [group * half + j for j in range(half)] + [2 * half + jnp.bitwise_xor(me, rel)]
    views = []
    row = 0
    for j, head in enumerate(heads):
        for part in parts if rel < 2 or j == half else parts[:1]:
            pieces = [(0,)] if len(part.shape) == 3 else [(0, i) for i in range(part.shape[1])]
            for piece in pieces:
                count = part.shape[-2]
                source = part.at[(*piece, slice(None), head_cols(head))]
                views.append((source, out.at[pl.ds(row, count), :]))
                row += count
    return views


def pack_kernel(half, rels, *refs):
    scalars, parts = refs[:3], refs[3:8]
    mask_ref, list_ref, place_ref, sems = refs[-4:]
    out_refs = refs[-4 - len(rels) : -4]
    me = lax.axis_index("seq")
    views = list(zip(scalars, (mask_ref, list_ref, place_ref)))[: 3 if 0 in rels else 1]
    used = len(views)
    for rel, out in zip(rels, out_refs):
        views += pack_copies(half, rel, me, parts, out)
    copies = [
        pltpu.make_async_copy(source, target, sems.at[i])
        for i, (source, target) in enumerate(views)
    ]
    for copy in copies:
        copy.start()
    for copy in copies[:used]:
        copy.wait()
    for rel, out in zip(rels, out_refs):
        other = jnp.bitwise_xor(me, rel)
        ident = lax.broadcasted_iota(jnp.int32, (FLAG_ROWS, HD), 0)
        block = jnp.zeros((FLAG_ROWS, HD), F32)
        for key in range(4):
            live = mask_ref[0, 0, jnp.bitwise_xor(other, key)] > 0
            block = jnp.where(ident == key, fill(live), block)
        if rel == 0:
            frames = parts[3].shape[1]
            for key, value in enumerate(frame_fills(place_ref, list_ref, me, frames), 4):
                block = jnp.where(ident == key, value, block)
        row = out.shape[0] - FLAG_ROWS
        out[row : row + FLAG_ROWS, :] = block.astype(BF16)
    for copy in copies[used:]:
        copy.wait()


def eights(block, reduce):
    return reduce(block.reshape(block.shape[0] // 8, 8, block.shape[1]), axis=0)


def softmax(scores, fills):
    peak = None
    row = 0
    for count, value in fills:
        block = eights(scores[row : row + count, :], jnp.max) * FACTOR + value
        peak = block if peak is None else jnp.maximum(peak, block)
        row += count
    peak = jnp.max(peak, axis=0, keepdims=True)
    weights = []
    total = None
    row = 0
    for count, value in fills:
        block = jnp.exp2(scores[row : row + count, :] * FACTOR - (peak - 2.0 * value))
        part = eights(block, jnp.sum)
        total = part if total is None else total + part
        weights.append(block.astype(BF16))
        row += count
    total = jnp.sum(total, axis=0, keepdims=True)
    total = jnp.where(total == 0.0, 1.0, total)
    return jnp.concatenate(weights, axis=0), 1.0 / total, peak + jnp.log2(total)


def all_fills(refs, frames, frame_tok):
    blocks = []
    for ref in refs:
        row = ref.shape[0] - FLAG_ROWS
        blocks.append(ref[row : row + FLAG_ROWS, :].astype(F32))
    fills = [
        (TILE, jnp.concatenate([block[key : key + 1, :] for block in blocks], axis=1))
        for key in range(4)
    ]
    for key in range(4, 4 + 4 * frames):
        row = blocks[0][key : key + 1, :]
        fills.append((frame_tok, jnp.concatenate([row] * len(refs), axis=1)))
    return fills


def stack(places, start, count):
    return jnp.concatenate(
        [ref[base + start : base + start + count, :] for ref, base in places], axis=0
    )


def attend_parts(tasks, cache):
    scores = []
    for query_places, key_places, _ in tasks:
        key_rows = jnp.concatenate(
            [stack(key_places, TILE, TILE), stack(key_places, 3 * TILE, cache)], axis=0
        )
        scores.append(
            lax.dot_general(
                key_rows, stack(query_places, 0, TILE), (((1,), (1,)), ((), ())),
                preferred_element_type=F32,
            )
        )
    softmaxed = [softmax(block, fills) for block, (_, _, fills) in zip(scores, tasks)]
    out = []
    for (weights, scale, logs), (_, key_places, _) in zip(softmaxed, tasks):
        value_rows = jnp.concatenate(
            [stack(key_places, 2 * TILE, TILE), stack(key_places, 3 * TILE + cache, cache)], axis=0
        )
        summed = lax.dot_general(
            value_rows, weights, (((0,), (0,)), ((), ())), preferred_element_type=F32
        )
        out.append((summed * scale, logs))
    return out


def three_parts(row):
    parts = []
    for _ in range(3):
        part = row.astype(BF16).astype(F32)
        parts.append(part)
        row = row - part
    return parts


def stat_block(rows):
    spare = FLAG_ROWS - len(rows)
    return jnp.concatenate(rows + [jnp.zeros((spare, TILE), F32)], axis=0).astype(BF16)


def early_kernel(
    half, frames, frame_tok, near0_ref, near1_ref, far3_ref,
    own_ref, own_log_ref, out1_ref, out3_ref,
):
    cache = frames * frame_tok
    span = 3 * TILE + 2 * cache
    fills = all_fills((near0_ref, near1_ref, far3_ref), frames, frame_tok)
    fills = fills[:2] + fills[4 : 4 + 2 * frames]
    tasks = []
    for j in range(half):
        pair = ((near0_ref, j * span), (near1_ref, j * span))
        tasks.append((pair + ((far3_ref, j * TILE),), pair, fills))
    stats = [[], []]
    outs = (out1_ref, out3_ref)
    for j, (summed, logs) in enumerate(attend_parts(tasks, cache)):
        rows = slice(j * HD, (j + 1) * HD)
        own_ref[rows, :] = summed[:, :TILE]
        own_log_ref[j : j + 1, :] = logs[:, :TILE]
        for i, out in enumerate(outs):
            cols = slice((i + 1) * TILE, (i + 2) * TILE)
            out[rows, :] = summed[:, cols].astype(BF16)
            stats[i] += three_parts(logs[:, cols])
    for i, out in enumerate(outs):
        row = half * HD
        out[row : row + FLAG_ROWS, :] = stat_block(stats[i])
        row += FLAG_ROWS
        out[row:, :] = jnp.zeros((out.shape[0] - row, TILE), BF16)


def late_kernel(
    half, frames, frame_tok, near0_ref, near1_ref, far3_ref, far2_ref, before_ref,
    out2_ref, *whole_refs,
):
    del before_ref
    cache = frames * frame_tok
    span = 3 * TILE + 2 * cache
    ins = (near0_ref, near1_ref, far2_ref, far3_ref)
    fills = all_fills(ins, frames, frame_tok)
    cols = slice(2 * TILE, 3 * TILE)
    pair_fills = [
        (count, value[:, cols]) for count, value in fills[:2] + fills[4 : 4 + 2 * frames]
    ]
    tasks = []
    for j in range(half):
        pair = ((near0_ref, j * span), (near1_ref, j * span))
        tasks.append((((far2_ref, j * TILE),), pair, pair_fills))
    places = [(ref, half * span) for ref in ins[:2]] + [(ref, half * TILE) for ref in ins[2:]]
    tasks.append((places, places, fills))
    *parts, (whole, _) = attend_parts(tasks, cache)
    stats = []
    for j, (summed, logs) in enumerate(parts):
        out2_ref[j * HD : (j + 1) * HD, :] = summed.astype(BF16)
        stats += three_parts(logs)
    row = half * HD
    out2_ref[row : row + FLAG_ROWS, :] = stat_block(stats)
    for rel, out in enumerate(whole_refs):
        out[...] = whole[:, rel * TILE : (rel + 1) * TILE].astype(BF16)


def joined(half, j, first, first_log, second_ref):
    start = half * HD
    block = second_ref[start : start + FLAG_ROWS, :].astype(F32)
    row = 3 * j
    second_log = block[row : row + 1, :] + block[row + 1 : row + 2, :] + block[row + 2 : row + 3, :]
    second = second_ref[j * HD : (j + 1) * HD, :].astype(F32)
    peak = jnp.maximum(first_log, second_log)
    first_weight = jnp.exp2(first_log - peak)
    second_weight = jnp.exp2(second_log - peak)
    scale = 1.0 / (first_weight + second_weight)
    both = first * (first_weight * scale) + second * (second_weight * scale)
    return both.astype(BF16).T


def far_kernel(half, in3_ref, in1_ref, out_ref):
    block = in1_ref[half * HD : half * HD + FLAG_ROWS, :].astype(F32)
    for j in range(half):
        row = 3 * j
        log = block[row : row + 1, :] + block[row + 1 : row + 2, :] + block[row + 2 : row + 3, :]
        rows = slice(j * HD, (j + 1) * HD)
        out_ref[:, rows] = joined(half, j, in1_ref[rows, :].astype(F32), log, in3_ref)


def merge_kernel(
    half, own_ref, own_log_ref, far_ref, in2_ref,
    whole0_ref, whole2_ref, whole3_ref, whole1_ref, out_hbm, split_ref, whole_ref, sems,
):
    me = lax.axis_index("seq")
    side = lax.rem(me, 2)
    copies = []

    def leave(block_ref, head):
        cols = pl.ds(pl.multiple_of(head * HD, HD), block_ref.shape[1])
        copy = pltpu.make_async_copy(block_ref, out_hbm.at[0, :, cols], sems.at[len(copies)])
        copy.start()
        copies.append(copy)

    leave(far_ref, (1 - side) * half)
    for rel, ref in enumerate((whole0_ref, whole1_ref, whole2_ref, whole3_ref)):
        whole_ref[:, head_cols(jnp.bitwise_xor(me, rel))] = ref[...].T
    leave(whole_ref, 2 * half)
    for j in range(half):
        rows = slice(j * HD, (j + 1) * HD)
        split_ref[:, rows] = joined(
            half, j, own_ref[rows, :], own_log_ref[j : j + 1, :], in2_ref
        )
    leave(split_ref, side * half)
    for copy in copies:
        copy.wait()


def send(array, rel):
    return lax.ppermute(array, "seq", [(i, i ^ rel) for i in range(4)])


def near(array):
    return pltpu.with_memory_space_constraint(array, pltpu.VMEM)


def exchanged(queries, keys, values, cache_keys, cache_values, frame_list, frame_place, tile_mask):
    head_count = queries.shape[2] // HD
    half = (head_count - 4) // 2
    frames, frame_tok = cache_keys.shape[1:3]
    span = 3 * TILE + 2 * frames * frame_tok
    pair_rows = (half + 1) * span + FLAG_ROWS
    far_rows = half * TILE + span + FLAG_ROWS
    back_rows = half * HD + FLAG_ROWS
    scalars = [pltpu.SMEM(array.shape, jnp.int32) for array in (tile_mask, frame_list, frame_place)]
    once = [pl.BlockSpec(memory_space=pl.ANY)]
    arrays = (tile_mask, frame_list, frame_place, queries, keys, values, cache_keys, cache_values)
    near1 = pl.pallas_call(
        functools.partial(pack_kernel, half, (1,)),
        out_shape=pltpu.VMEM((pair_rows, HD), BF16),
        in_specs=once * 8,
        out_specs=VMEM,
        scratch_shapes=scalars + [pltpu.SemaphoreType.DMA((3 + (half + 1) * (3 + 2 * frames),))],
    )(*arrays)
    far3, far2 = pl.pallas_call(
        functools.partial(pack_kernel, half, (3, 2)),
        out_shape=(pltpu.VMEM((far_rows, HD), BF16),) * 2,
        in_specs=once * 9,
        out_specs=(VMEM,) * 2,
        scratch_shapes=scalars + [pltpu.SemaphoreType.DMA((3 + 2 * (half + 3 + 2 * frames),))],
    )(*arrays, near(near1))
    near0 = pl.pallas_call(
        functools.partial(pack_kernel, half, (0,)),
        out_shape=pltpu.VMEM((pair_rows, HD), BF16),
        in_specs=once * 9,
        out_specs=VMEM,
        scratch_shapes=scalars + [pltpu.SemaphoreType.DMA((3 + (half + 1) * (3 + 2 * frames),))],
    )(*arrays, near(far2))
    near0, near1 = near(near0), near(send(near1, 1))
    far3, far2 = near(send(far3, 3)), near(send(far2, 2))
    own, own_log, back1, back3 = pl.pallas_call(
        functools.partial(early_kernel, half, frames, frame_tok),
        out_shape=(
            pltpu.VMEM((half * HD, TILE), F32),
            pltpu.VMEM((half, TILE), F32),
        ) + (pltpu.VMEM((back_rows + 8, TILE), BF16),) * 2,
        in_specs=[VMEM] * 3,
        out_specs=(VMEM,) * 4,
    )(near0, near1, far3)
    back3, back1 = near(send(back3, 3)), near(send(back1, 1))
    back2, *whole = pl.pallas_call(
        functools.partial(late_kernel, half, frames, frame_tok),
        out_shape=(pltpu.VMEM((back_rows, TILE), BF16),)
        + (pltpu.VMEM((HD, TILE), BF16),) * 4,
        in_specs=[VMEM] * 5,
        out_specs=(VMEM,) * 5,
    )(near0, near1, far3, far2, near(own_log))
    back2 = near(send(back2, 2))
    whole = [near(whole[0])] + [near(send(whole[rel], rel)) for rel in (2, 3, 1)]
    far = pl.pallas_call(
        functools.partial(far_kernel, half),
        out_shape=pltpu.VMEM((TILE, half * HD), BF16),
        in_specs=[VMEM] * 2,
        out_specs=VMEM,
    )(back3, back1)
    return pl.pallas_call(
        functools.partial(merge_kernel, half),
        out_shape=jax.ShapeDtypeStruct(queries.shape, BF16),
        in_specs=[VMEM] * 8,
        out_specs=pl.BlockSpec(memory_space=pl.ANY),
        scratch_shapes=[
            pltpu.VMEM((TILE, half * HD), BF16),
            pltpu.VMEM((TILE, 4 * HD), BF16),
            pltpu.SemaphoreType.DMA((3,)),
        ],
    )(near(own), near(own_log), near(far), back2, *whole)


def body(queries, keys, values, cache_keys, cache_values, frame_list, frame_place, tile_mask):
    head_count = queries.shape[2] // HD
    fits = (
        lax.axis_size("seq") == 4
        and queries.shape[0] == 1
        and queries.shape[1] == TILE
        and head_count % 2 == 0
        and 6 <= head_count <= 14
        and 4 + 4 * cache_keys.shape[1] <= FLAG_ROWS
    )
    run = exchanged if fits else gathered
    return run(queries, keys, values, cache_keys, cache_values, frame_list, frame_place, tile_mask)


def solution(mesh):
    return jax.shard_map(
        body,
        mesh=mesh,
        in_specs=(
            P(("groups", "batch"), "seq", "head"),
            P(("groups", "batch"), "seq", "head"),
            P(("groups", "batch"), "seq", "head"),
            P(("groups", "batch"), "seq", None, "head"),
            P(("groups", "batch"), "seq", None, "head"),
            P(("groups", "batch"), None),
            P(("groups", "batch"), None),
            P(("groups", "batch"), "seq", None),
        ),
        out_specs=P(("groups", "batch"), "seq", "head"),
        check_vma=False,
    )
```

```python
import functools
import math

import jax
import jax.numpy as jnp
from jax import lax
from jax.experimental import pallas as pl
from jax.experimental.pallas import tpu as pltpu
from jax.sharding import PartitionSpec as P

HD = 128
TILE = 128
NEG_FILL = -1e30
FACTOR = math.log2(math.e) / math.sqrt(HD)
FLAG_ROWS = 16
VMEM = pl.BlockSpec(memory_space=pltpu.VMEM)
SMEM = pl.BlockSpec(memory_space=pltpu.SMEM)
BF16 = jnp.bfloat16
F32 = jnp.float32


def attend(running, key_part, value_part, live, query_heads):
    videos, length, col_count = key_part.shape
    head_count = col_count // HD

    def update(previous):
        peak_old, total_old, summed_old = previous
        key_heads = key_part.reshape(videos, length, head_count, HD)
        value_heads = value_part.reshape(videos, length, head_count, HD)
        scores = jnp.einsum(
            "vqhd,vkhd->vhqk", query_heads, key_heads, preferred_element_type=jnp.float32
        ) * (1.0 / math.sqrt(HD))
        allowed = live[:, None, :, :]
        scores = jnp.where(allowed, scores, NEG_FILL)
        peak_new = jnp.maximum(peak_old, jnp.max(scores, axis=3))
        weights = jnp.where(allowed, jnp.exp(scores - peak_new[..., None]), 0.0)
        factor = jnp.exp(peak_old - peak_new)
        total_new = total_old * factor + jnp.sum(weights, axis=3)
        product = jnp.einsum(
            "vhqk,vkhd->vhqd",
            weights.astype(jnp.bfloat16),
            value_heads,
            preferred_element_type=jnp.float32,
        )
        summed_new = summed_old * factor[..., None] + product
        return (peak_new, total_new, summed_new)

    def unchanged(previous):
        return previous

    return lax.cond(jnp.any(live), update, unchanged, running)


def gathered(queries, keys, values, cache_keys, cache_values, frame_list, frame_place, tile_mask):
    videos, tok_rows, col_count = queries.shape
    head_count = col_count // HD
    query_heads = queries.reshape(videos, tok_rows, head_count, HD)
    running = (
        jnp.full((videos, head_count, tok_rows), NEG_FILL, jnp.float32),
        jnp.zeros((videos, head_count, tok_rows), jnp.float32),
        jnp.zeros((videos, head_count, tok_rows, HD), jnp.float32),
    )
    frame_tok = cache_keys.shape[2]
    listed = jnp.any(frame_place[:, :, None] == frame_list[:, None, :], axis=2)
    key_piece = lax.all_gather(cache_keys, "seq", axis=1, tiled=True)
    value_piece = lax.all_gather(cache_values, "seq", axis=1, tiled=True)
    count_frames = key_piece.shape[1]
    token_flags = jnp.repeat(listed, frame_tok, axis=1)
    live = jnp.broadcast_to(token_flags[:, None, :], (videos, tok_rows, count_frames * frame_tok))
    key_flat = key_piece.reshape(videos, count_frames * frame_tok, col_count)
    value_flat = value_piece.reshape(videos, count_frames * frame_tok, col_count)
    running = attend(running, key_flat, value_flat, live, query_heads)
    key_piece = lax.all_gather(keys, "seq", axis=1, tiled=True)
    value_piece = lax.all_gather(values, "seq", axis=1, tiled=True)
    length = key_piece.shape[1]
    key_tiles = jnp.arange(length, dtype=jnp.int32) // TILE
    tile_live = jnp.take(tile_mask, key_tiles, axis=2)
    running = attend(
        running, key_piece, value_piece, jnp.repeat(tile_live, TILE, axis=1) > 0, query_heads
    )
    peak, total, summed = running
    result = summed / total[..., None]
    return result.transpose(0, 2, 1, 3).reshape(videos, tok_rows, col_count).astype(jnp.bfloat16)


def head_cols(head):
    start = head * HD
    if not isinstance(head, int):
        start = pl.multiple_of(start, HD)
    return pl.ds(start, HD)


def fill(live):
    return jnp.where(live, 0.0, NEG_FILL)


def frame_fills(place_ref, list_ref, me, frames):
    out = []
    for rel in range(4):
        for slot in range(frames):
            held = place_ref[0, jnp.bitwise_xor(me, rel) * frames + slot]
            live = held == list_ref[0, 0]
            for entry in range(1, list_ref.shape[1]):
                live = live | (held == list_ref[0, entry])
            out.append(fill(live))
    return out


def rows_of(ref, head):
    if len(ref.shape) == 3:
        return ref[0, :, head_cols(head)]
    return ref[0, :, :, head_cols(head)].reshape(ref.shape[1] * ref.shape[2], HD)


def put(out, row, refs, head):
    for ref in refs:
        block = rows_of(ref, head)
        out[row : row + block.shape[0], :] = block
        row += block.shape[0]
    return row


def pack_copies(half, rel, me, parts, out):
    side = lax.rem(me, 2)
    group = (1 - side) if rel % 2 else side
    heads = [group * half + j for j in range(half)] + [2 * half + jnp.bitwise_xor(me, rel)]
    views = []
    row = 0
    for j, head in enumerate(heads):
        for part in parts if rel < 2 or j == half else parts[:1]:
            pieces = [(0,)] if len(part.shape) == 3 else [(0, i) for i in range(part.shape[1])]
            for piece in pieces:
                count = part.shape[-2]
                source = part.at[(*piece, slice(None), head_cols(head))]
                views.append((source, out.at[pl.ds(row, count), :]))
                row += count
    return views


def pack_kernel(half, rels, *refs):
    scalars, parts = refs[:3], refs[3:8]
    mask_ref, list_ref, place_ref, sems = refs[-4:]
    out_refs = refs[-4 - len(rels) : -4]
    me = lax.axis_index("seq")
    views = list(zip(scalars, (mask_ref, list_ref, place_ref)))[: 3 if 0 in rels else 1]
    used = len(views)
    for rel, out in zip(rels, out_refs):
        views += pack_copies(half, rel, me, parts, out)
    copies = [
        pltpu.make_async_copy(source, target, sems.at[i])
        for i, (source, target) in enumerate(views)
    ]
    for copy in copies:
        copy.start()
    for copy in copies[:used]:
        copy.wait()
    for rel, out in zip(rels, out_refs):
        other = jnp.bitwise_xor(me, rel)
        ident = lax.broadcasted_iota(jnp.int32, (FLAG_ROWS, HD), 0)
        block = jnp.zeros((FLAG_ROWS, HD), F32)
        for key in range(4):
            live = mask_ref[0, 0, jnp.bitwise_xor(other, key)] > 0
            block = jnp.where(ident == key, fill(live), block)
        if rel == 0:
            frames = parts[3].shape[1]
            for key, value in enumerate(frame_fills(place_ref, list_ref, me, frames), 4):
                block = jnp.where(ident == key, value, block)
        row = out.shape[0] - FLAG_ROWS
        out[row : row + FLAG_ROWS, :] = block.astype(BF16)
    for copy in copies[used:]:
        copy.wait()


def eights(block, reduce):
    return reduce(block.reshape(block.shape[0] // 8, 8, block.shape[1]), axis=0)


def softmax(scores, fills):
    peak = None
    row = 0
    for count, value in fills:
        block = eights(scores[row : row + count, :], jnp.max) * FACTOR + value
        peak = block if peak is None else jnp.maximum(peak, block)
        row += count
    peak = jnp.max(peak, axis=0, keepdims=True)
    weights = []
    total = None
    row = 0
    for count, value in fills:
        block = jnp.exp2(scores[row : row + count, :] * FACTOR - (peak - 2.0 * value))
        part = eights(block, jnp.sum)
        total = part if total is None else total + part
        weights.append(block.astype(BF16))
        row += count
    total = jnp.sum(total, axis=0, keepdims=True)
    total = jnp.where(total == 0.0, 1.0, total)
    return jnp.concatenate(weights, axis=0), 1.0 / total, peak + jnp.log2(total)


def all_fills(refs, frames, frame_tok):
    blocks = []
    for ref in refs:
        row = ref.shape[0] - FLAG_ROWS
        blocks.append(ref[row : row + FLAG_ROWS, :].astype(F32))
    fills = [
        (TILE, jnp.concatenate([block[key : key + 1, :] for block in blocks], axis=1))
        for key in range(4)
    ]
    for key in range(4, 4 + 4 * frames):
        row = blocks[0][key : key + 1, :]
        fills.append((frame_tok, jnp.concatenate([row] * len(refs), axis=1)))
    return fills


def stack(places, start, count):
    return jnp.concatenate(
        [ref[base + start : base + start + count, :] for ref, base in places], axis=0
    )


def attend_parts(tasks, cache):
    scores = []
    for query_places, key_places, _ in tasks:
        key_rows = jnp.concatenate(
            [stack(key_places, TILE, TILE), stack(key_places, 3 * TILE, cache)], axis=0
        )
        scores.append(
            lax.dot_general(
                key_rows, stack(query_places, 0, TILE), (((1,), (1,)), ((), ())),
                preferred_element_type=F32,
            )
        )
    softmaxed = [softmax(block, fills) for block, (_, _, fills) in zip(scores, tasks)]
    out = []
    for (weights, scale, logs), (_, key_places, _) in zip(softmaxed, tasks):
        value_rows = jnp.concatenate(
            [stack(key_places, 2 * TILE, TILE), stack(key_places, 3 * TILE + cache, cache)], axis=0
        )
        summed = lax.dot_general(
            value_rows, weights, (((0,), (0,)), ((), ())), preferred_element_type=F32
        )
        out.append((summed * scale, logs))
    return out


def three_parts(row):
    parts = []
    for _ in range(3):
        part = row.astype(BF16).astype(F32)
        parts.append(part)
        row = row - part
    return parts


def stat_block(rows):
    spare = FLAG_ROWS - len(rows)
    return jnp.concatenate(rows + [jnp.zeros((spare, TILE), F32)], axis=0).astype(BF16)


def early_kernel(
    half, frames, frame_tok, near0_ref, near1_ref, far3_ref,
    own_ref, own_log_ref, out1_ref, out3_ref,
):
    cache = frames * frame_tok
    span = 3 * TILE + 2 * cache
    fills = all_fills((near0_ref, near1_ref, far3_ref), frames, frame_tok)
    fills = fills[:2] + fills[4 : 4 + 2 * frames]
    tasks = []
    for j in range(half):
        pair = ((near0_ref, j * span), (near1_ref, j * span))
        tasks.append((pair + ((far3_ref, j * TILE),), pair, fills))
    stats = [[], []]
    outs = (out1_ref, out3_ref)
    for j, (summed, logs) in enumerate(attend_parts(tasks, cache)):
        rows = slice(j * HD, (j + 1) * HD)
        own_ref[rows, :] = summed[:, :TILE]
        own_log_ref[j : j + 1, :] = logs[:, :TILE]
        for i, out in enumerate(outs):
            cols = slice((i + 1) * TILE, (i + 2) * TILE)
            out[rows, :] = summed[:, cols].astype(BF16)
            stats[i] += three_parts(logs[:, cols])
    for i, out in enumerate(outs):
        row = half * HD
        out[row : row + FLAG_ROWS, :] = stat_block(stats[i])
        row += FLAG_ROWS
        if row < out.shape[0]:
            out[row:, :] = jnp.zeros((out.shape[0] - row, TILE), BF16)


def late_kernel(
    half, frames, frame_tok, near0_ref, near1_ref, far3_ref, far2_ref, early1_ref,
    out2_ref, out1_ref, *whole_refs,
):
    out1_ref[...] = early1_ref[...]
    cache = frames * frame_tok
    span = 3 * TILE + 2 * cache
    ins = (near0_ref, near1_ref, far2_ref, far3_ref)
    fills = all_fills(ins, frames, frame_tok)
    cols = slice(2 * TILE, 3 * TILE)
    pair_fills = [
        (count, value[:, cols]) for count, value in fills[:2] + fills[4 : 4 + 2 * frames]
    ]
    tasks = []
    for j in range(half):
        pair = ((near0_ref, j * span), (near1_ref, j * span))
        tasks.append((((far2_ref, j * TILE),), pair, pair_fills))
    places = [(ref, half * span) for ref in ins[:2]] + [(ref, half * TILE) for ref in ins[2:]]
    tasks.append((places, places, fills))
    *parts, (whole, _) = attend_parts(tasks, cache)
    stats = []
    for j, (summed, logs) in enumerate(parts):
        out2_ref[j * HD : (j + 1) * HD, :] = summed.astype(BF16)
        stats += three_parts(logs)
    row = half * HD
    out2_ref[row : row + FLAG_ROWS, :] = stat_block(stats)
    for rel, out in enumerate(whole_refs):
        out[...] = whole[:, rel * TILE : (rel + 1) * TILE].astype(BF16)


def joined(half, j, first, first_log, second_ref):
    start = half * HD
    block = second_ref[start : start + FLAG_ROWS, :].astype(F32)
    row = 3 * j
    second_log = block[row : row + 1, :] + block[row + 1 : row + 2, :] + block[row + 2 : row + 3, :]
    second = second_ref[j * HD : (j + 1) * HD, :].astype(F32)
    peak = jnp.maximum(first_log, second_log)
    first_weight = jnp.exp2(first_log - peak)
    second_weight = jnp.exp2(second_log - peak)
    scale = 1.0 / (first_weight + second_weight)
    both = first * (first_weight * scale) + second * (second_weight * scale)
    return both.astype(BF16).T


def keep_kernel(in3_ref, out_ref):
    out_ref[...] = in3_ref[: out_ref.shape[0], :]


def merge_kernel(
    half, own_ref, own_log_ref, in3_ref, in2_ref, in1_ref,
    whole0_ref, whole2_ref, whole3_ref, whole1_ref, out_hbm, far_ref, split_ref, whole_ref, sems,
):
    me = lax.axis_index("seq")
    side = lax.rem(me, 2)
    copies = []

    def leave(block_ref, head):
        cols = pl.ds(pl.multiple_of(head * HD, HD), block_ref.shape[1])
        copy = pltpu.make_async_copy(block_ref, out_hbm.at[0, :, cols], sems.at[len(copies)])
        copy.start()
        copies.append(copy)

    block = in1_ref[half * HD : half * HD + FLAG_ROWS, :].astype(F32)
    for j in range(half):
        row = 3 * j
        log = block[row : row + 1, :] + block[row + 1 : row + 2, :] + block[row + 2 : row + 3, :]
        rows = slice(j * HD, (j + 1) * HD)
        far_ref[:, rows] = joined(half, j, in1_ref[rows, :].astype(F32), log, in3_ref)
    leave(far_ref, (1 - side) * half)
    for rel, ref in enumerate((whole0_ref, whole1_ref, whole2_ref, whole3_ref)):
        whole_ref[:, head_cols(jnp.bitwise_xor(me, rel))] = ref[...].T
    leave(whole_ref, 2 * half)
    for j in range(half):
        rows = slice(j * HD, (j + 1) * HD)
        split_ref[:, rows] = joined(
            half, j, own_ref[rows, :], own_log_ref[j : j + 1, :], in2_ref
        )
    leave(split_ref, side * half)
    for copy in copies:
        copy.wait()


def send(array, rel):
    return lax.ppermute(array, "seq", [(i, i ^ rel) for i in range(4)])


def near(array):
    return pltpu.with_memory_space_constraint(array, pltpu.VMEM)


def exchanged(queries, keys, values, cache_keys, cache_values, frame_list, frame_place, tile_mask):
    head_count = queries.shape[2] // HD
    half = (head_count - 4) // 2
    frames, frame_tok = cache_keys.shape[1:3]
    span = 3 * TILE + 2 * frames * frame_tok
    pair_rows = (half + 1) * span + FLAG_ROWS
    far_rows = half * TILE + span + FLAG_ROWS
    back_rows = half * HD + FLAG_ROWS
    scalars = [pltpu.SMEM(array.shape, jnp.int32) for array in (tile_mask, frame_list, frame_place)]
    once = [pl.BlockSpec(memory_space=pl.ANY)]
    arrays = (tile_mask, frame_list, frame_place, queries, keys, values, cache_keys, cache_values)
    near1 = pl.pallas_call(
        functools.partial(pack_kernel, half, (1,)),
        out_shape=pltpu.VMEM((pair_rows, HD), BF16),
        in_specs=once * 8,
        out_specs=VMEM,
        scratch_shapes=scalars + [pltpu.SemaphoreType.DMA((3 + (half + 1) * (3 + 2 * frames),))],
    )(*arrays)
    far3, far2 = pl.pallas_call(
        functools.partial(pack_kernel, half, (3, 2)),
        out_shape=(pltpu.VMEM((far_rows, HD), BF16),) * 2,
        in_specs=once * 9,
        out_specs=(VMEM,) * 2,
        scratch_shapes=scalars + [pltpu.SemaphoreType.DMA((3 + 2 * (half + 3 + 2 * frames),))],
    )(*arrays, near(near1))
    near0 = pl.pallas_call(
        functools.partial(pack_kernel, half, (0,)),
        out_shape=pltpu.VMEM((pair_rows, HD), BF16),
        in_specs=once * 9,
        out_specs=VMEM,
        scratch_shapes=scalars + [pltpu.SemaphoreType.DMA((3 + (half + 1) * (3 + 2 * frames),))],
    )(*arrays, near(far2))
    near0, near1 = near(near0), near(send(near1, 1))
    far3, far2 = near(send(far3, 3)), near(send(far2, 2))
    own, own_log, back1, back3 = pl.pallas_call(
        functools.partial(early_kernel, half, frames, frame_tok),
        out_shape=(
            pltpu.VMEM((half * HD, TILE), F32),
            pltpu.VMEM((half, TILE), F32),
        ) + (pltpu.VMEM((back_rows, TILE), BF16), pltpu.VMEM((back_rows + 8, TILE), BF16)),
        in_specs=[VMEM] * 3,
        out_specs=(VMEM,) * 4,
    )(near0, near1, far3)
    back3 = near(send(back3, 3))
    back2, back1, *whole = pl.pallas_call(
        functools.partial(late_kernel, half, frames, frame_tok),
        out_shape=(pltpu.VMEM((back_rows, TILE), BF16),) * 2
        + (pltpu.VMEM((HD, TILE), BF16),) * 4,
        in_specs=[VMEM] * 5,
        out_specs=(VMEM,) * 6,
    )(near0, near1, far3, far2, near(back1))
    back2, back1 = near(send(back2, 2)), near(send(back1, 1))
    whole = [near(whole[0])] + [near(send(whole[rel], rel)) for rel in (2, 3, 1)]
    kept3 = pl.pallas_call(
        keep_kernel,
        out_shape=pltpu.VMEM((back_rows, TILE), BF16),
        in_specs=[VMEM],
        out_specs=VMEM,
    )(back3)
    return pl.pallas_call(
        functools.partial(merge_kernel, half),
        out_shape=jax.ShapeDtypeStruct(queries.shape, BF16),
        in_specs=[VMEM] * 9,
        out_specs=pl.BlockSpec(memory_space=pl.ANY),
        scratch_shapes=[
            pltpu.VMEM((TILE, half * HD), BF16),
            pltpu.VMEM((TILE, half * HD), BF16),
            pltpu.VMEM((TILE, 4 * HD), BF16),
            pltpu.SemaphoreType.DMA((3,)),
        ],
    )(near(own), near(own_log), near(kept3), back2, back1, *whole)


def body(queries, keys, values, cache_keys, cache_values, frame_list, frame_place, tile_mask):
    head_count = queries.shape[2] // HD
    fits = (
        lax.axis_size("seq") == 4
        and queries.shape[0] == 1
        and queries.shape[1] == TILE
        and head_count % 2 == 0
        and 6 <= head_count <= 14
        and 4 + 4 * cache_keys.shape[1] <= FLAG_ROWS
    )
    run = exchanged if fits else gathered
    return run(queries, keys, values, cache_keys, cache_values, frame_list, frame_place, tile_mask)


def solution(mesh):
    return jax.shard_map(
        body,
        mesh=mesh,
        in_specs=(
            P(("groups", "batch"), "seq", "head"),
            P(("groups", "batch"), "seq", "head"),
            P(("groups", "batch"), "seq", "head"),
            P(("groups", "batch"), "seq", None, "head"),
            P(("groups", "batch"), "seq", None, "head"),
            P(("groups", "batch"), None),
            P(("groups", "batch"), None),
            P(("groups", "batch"), "seq", None),
        ),
        out_specs=P(("groups", "batch"), "seq", "head"),
        check_vma=False,
    )
```
